32 devices in a mesh: fsdp: 4 (over z), emb: 8 (over y, x, core).
Axes of the slice: x: 2, y: 2, z: 4, core: 2. Of those that a mesh axis runs over, the one named last changes fastest.
Arguments:
- item_table: float32 [131072, 256], P(('fsdp', 'emb')), may hold values from -6 to 6
- item_owner: int32 [32, 1024, 1], P(('fsdp', 'emb')), may hold values from 0 to 31; in each aligned block of 1024 rows (0 to 1023, 1024 to 2047, ..., all dimensions but the last counted through in order) at most 64 rows name the same one
- item_row: int32 [32, 1024], P(('fsdp', 'emb')), may hold values from 0 to 4095
- staleness: int32 [131072], P(('fsdp', 'emb')), may hold values from 0 to 3
- w_proj: bfloat16 [2, 256, 1024], P(None, 'fsdp'), may hold values from -0.375 to 0.375
- w_out: bfloat16 [2, 256, 256], P(None, 'fsdp'), may hold values from -0.375 to 0.375
- out_grad: bfloat16 [32, 1024, 256], P(('fsdp', 'emb')), may hold values from -6 to 6
Outputs:
- new_table: float32 [131072, 256], P(('fsdp', 'emb'))
- w_proj_grad: float32 [2, 256, 1024], P(None, 'fsdp')
- w_out_grad: float32 [2, 256, 256], P(None, 'fsdp')
The draws below stay inside these ranges and needn't reach their ends.
Inputs may be any that keep to these rules, and one draw needn't show every extreme that they name: `item_owner`: in each user's history no owner is named more than 64 times, a bound that some block reaches in every draw.
All inputs are finite; a program needn't handle non-finite values.
Results may differ from the reference program's by a relative error of at most 0.023.
Values may be sent and summed in bfloat16 or wider, within the bound.
No kernel may reach another device: no remote copies, remote signals or barrier semaphores. Data moves between devices by JAX's collectives and lax.ppermute only.
A program may use at most 128 MiB of HBM per device.

```python
import math
import jax
import jax.numpy as jnp
import numpy as np
from jax import lax

D = 256
HEADS = 4
DH = 64
HD = 256
LAYERS = 2
SEQ = 1024
ROWS_OWN = 4096
USERS = 32
CAP = 64
ITEMS = 131072
N_FSDP = 4
N_EMB = 8


def set_ends(array, stream_key, low, largest):
    spot = [jax.random.randint(jax.random.fold_in(stream_key, axis), (), 0, length) for axis, length in enumerate(array.shape)]
    longest = array.shape.index(max(array.shape))
    next_to = spot[:longest] + [(spot[longest] + 1) % array.shape[longest]] + spot[longest + 1:]
    return array.at[tuple(spot)].set(low).at[tuple(next_to)].set(largest)


def steps_of(key, dims, split, least, largest):
    gain, own = 1.0, jax.random.fold_in(key, 6)
    for axis_at, blocks in split:
        steps = jnp.exp(jax.random.uniform(jax.random.fold_in(own, axis_at), (blocks,), jnp.float32, least / len(split), largest / len(split)))
        gain = gain * jnp.repeat(steps, dims[axis_at] // blocks).reshape([-1 if axis == axis_at else 1 for axis in range(len(dims))])
    return gain


def rank_table(amount, slope):
    weights = [(1 << 20) // math.isqrt(grade ** slope) + 1 for grade in range(1, amount + 1)]
    deviation = 1 + sum(weights) // (1 << 30)
    return np.cumsum(np.array([max(1, weight // deviation) for weight in weights]))


def skewed_ids(key, extent, amount, skew):
    grid = rank_table(amount, skew)
    pick = jax.random.randint(jax.random.fold_in(key, 1), extent, 0, int(grid[amount - 1]))
    rank = jnp.searchsorted(jnp.asarray(grid, jnp.int32), pick, side="right")
    return jax.random.permutation(jax.random.fold_in(key, 2), amount)[rank].astype(jnp.int32)


def deal_out(rng, own, number, rows, number_of, top, bound, skew):
    order = jax.random.permutation(rng, number_of)
    crowded, ordinary = shares(number_of, rows * top, bound, skew, True), shares(number_of, rows * top, bound, skew, False)
    places = jnp.arange(number_of)

    def named(sizes, turn):
        used = int((sizes > 0).sum())
        fixed = max(1, used // 4)
        moved = fixed + (places - fixed + turn * (used - fixed)) % max(1, number_of - fixed)
        return jnp.zeros((number_of,), jnp.int32).at[order[jnp.where(places < fixed, places, moved)]].set(jnp.asarray(sizes, jnp.int32))

    sizes = jnp.where(number % 4 == 0, named(crowded, number // 4), named(ordinary, number - number // 4 - 1))
    mixed = jax.random.permutation(jax.random.fold_in(own, 3), number_of)
    donor, taker = mixed[0:number_of // 2 * 2:2], mixed[1:number_of // 2 * 2:2]
    room = jnp.minimum(sizes[donor] - 1, bound - sizes[taker]) // 2
    room = jnp.where((donor == order[0]) | (taker == order[0]) | (sizes[taker] == 0), 0, jnp.maximum(room, 0))
    moved = jax.random.randint(jax.random.fold_in(own, 4), (number_of // 2,), 0, 1 << 20) % (room + 1)
    sizes = sizes.at[donor].add(-moved).at[taker].add(moved)
    members = jnp.searchsorted(jnp.cumsum(sizes), jnp.arange(rows * top), side="right").astype(jnp.int32)
    table = members.reshape(top, rows).T
    table = table[jax.random.permutation(jax.random.fold_in(own, 1), rows)]
    turn = jax.random.randint(jax.random.fold_in(own, 2), (rows, 1), 0, top)
    return jnp.take_along_axis(table, (jnp.arange(top)[None, :] + turn) % top, axis=1)


def shares(amount, total, bound, slope, full):
    portions = [(1 << 20) // math.isqrt(standing ** slope) + 1 for standing in range(1, amount + 1)]
    largest = bound if full else min(bound, max(-(-total // amount), total * portions[0] // sum(portions)))
    least = 1 if total - largest >= amount - 1 else 0
    holding, surplus = [largest] + [least] * (amount - 1), total - largest - least * (amount - 1)
    while surplus > 0:
        movable = [i for i in range(1, amount) if holding[i] < largest] or [i for i in range(1, amount) if holding[i] < bound]
        pool, remaining = sum([portions[i] for i in movable]), surplus
        for i in movable:
            addition = min(bound - holding[i], max(1, remaining * portions[i] // pool), surplus)
            holding[i] = holding[i] + addition
            surplus = surplus - addition
    return np.array(holding)


def centred(rng, dims, deviation, limit, cuts=(), kind=jnp.bfloat16):
    gain = steps_of(rng, dims, cuts, -0.22, 0.18) if cuts else 1.0
    result = jax.random.normal(rng, dims, jnp.float32) * deviation * gain
    return jnp.minimum(jnp.maximum(result, -limit), limit).astype(kind)


def setup_inputs(seed: int = 0) -> dict:
    key_list = jax.random.split(jax.random.key(seed), 8)
    item_table = centred(key_list[0], (ITEMS, D), 1.0, 6.0, ((0, 32),), jnp.float32)
    item_owner_keys = jax.random.split(jax.random.fold_in(key_list[1], 1), USERS * SEQ // SEQ)
    item_owner_turns = jax.random.permutation(jax.random.fold_in(key_list[1], 3), USERS * SEQ // SEQ)
    item_owner = jax.vmap(lambda own, number: deal_out(jax.random.fold_in(key_list[1], 2), own, number, SEQ, USERS, 1, CAP, 2))(item_owner_keys, item_owner_turns).reshape((USERS, SEQ, 1))
    item_row = set_ends(skewed_ids(key_list[2], (USERS, SEQ), ROWS_OWN, 2), jax.random.fold_in(key_list[2], 3), 0, ROWS_OWN - 1).astype(jnp.int32)
    staleness = set_ends(jax.random.randint(key_list[3], (ITEMS,), 0, 4), jax.random.fold_in(key_list[3], 1), 0, 3).astype(jnp.int32)
    w_proj = centred(key_list[4], (LAYERS, D, 4 * HD), D ** -0.5, 0.375, ((1, 4),))
    w_out = centred(key_list[5], (LAYERS, HD, D), HD ** -0.5, 0.375, ((1, 4),))
    out_grad = centred(key_list[6], (USERS, SEQ, D), 1.0, 6.0, ((0, 32),))
    return dict(item_table=item_table, item_owner=item_owner, item_row=item_row, staleness=staleness, w_proj=w_proj, w_out=w_out, out_grad=out_grad)


EPSILON = 1e-05

def rounded(value):
    return lax.optimization_barrier(value.astype(jnp.bfloat16))

def normalize(value):
    center = value - lax.optimization_barrier(jnp.mean(value, axis=-1, keepdims=True))
    inverse = lax.rsqrt(lax.optimization_barrier(jnp.mean(center * center, axis=-1, keepdims=True)) + EPSILON)
    return (center * inverse, inverse)

def norm_back(gradient, normed, inverse):
    return inverse * (gradient - lax.optimization_barrier(jnp.mean(gradient, axis=-1, keepdims=True)) - normed * lax.optimization_barrier(jnp.mean(gradient * normed, axis=-1, keepdims=True)))

def silu_slope(value):
    logistic = jax.nn.sigmoid(value)
    return logistic * (1.0 + value * (1.0 - logistic))

def causal(first_row, block_rows, length):
    query_pos = first_row + lax.broadcasted_iota(jnp.int32, (block_rows, length), 0)
    key_pos = lax.broadcasted_iota(jnp.int32, (block_rows, length), 1)
    return key_pos <= query_pos

def layer_parts(hidden, proj_weight, out_weight):
    length = hidden.shape[0]
    hidden_float = hidden.astype(jnp.float32)
    normed_float, inverse_hidden = normalize(hidden_float)
    normed = rounded(normed_float)
    pre_act = jnp.dot(normed, proj_weight, preferred_element_type=jnp.float32)
    projected = rounded(jax.nn.silu(pre_act))
    width = out_weight.shape[0]
    gating = projected[:, :width]
    values = projected[:, width:2 * width].reshape(length, HEADS, DH)
    queries = projected[:, 2 * width:3 * width].reshape(length, HEADS, DH)
    key_rows = projected[:, 3 * width:].reshape(length, HEADS, DH)
    score_scale = DH ** (-0.5)
    scores = jnp.einsum('qhd,khd->hqk', queries.astype(jnp.float32), key_rows.astype(jnp.float32)) * score_scale
    visible = causal(0, length, length)[None]
    attn = rounded(jnp.where(visible, jax.nn.silu(scores), 0.0))
    mixture = jnp.einsum('hqk,khd->qhd', attn.astype(jnp.float32), values.astype(jnp.float32)).reshape(length, width)
    mix_normed, inverse_mix = normalize(mixture)
    gated_out = rounded(mix_normed * gating.astype(jnp.float32))
    return dict(hidden_float=hidden_float, normed_float=normed_float, inverse_hidden=inverse_hidden, normed=normed, pre_act=pre_act, gating=gating, values=values, queries=queries, key_rows=key_rows, scores=scores, visible=visible, attn=attn, mix_normed=mix_normed, inverse_mix=inverse_mix, gated_out=gated_out)

def layer_forward(hidden, proj_weight, out_weight):
    parts = layer_parts(hidden, proj_weight, out_weight)
    return rounded(parts['hidden_float'] + jnp.dot(parts['gated_out'], out_weight, preferred_element_type=jnp.float32))

def layer_backward(hidden, grad_out, proj_weight, out_weight):
    parts = layer_parts(hidden, proj_weight, out_weight)
    length = hidden.shape[0]
    width = out_weight.shape[0]
    score_scale = DH ** (-0.5)
    grad_round = rounded(grad_out)
    gw_out = jnp.dot(parts['gated_out'].T, grad_round, preferred_element_type=jnp.float32)
    grad_gated = jnp.dot(grad_round, out_weight.T, preferred_element_type=jnp.float32)
    grad_gate = grad_gated * parts['mix_normed']
    grad_mixture = norm_back(grad_gated * parts['gating'].astype(jnp.float32), parts['mix_normed'], parts['inverse_mix'])
    grad_mix = rounded(grad_mixture).reshape(length, HEADS, DH).astype(jnp.float32)
    values = parts['values'].astype(jnp.float32)
    queries = parts['queries'].astype(jnp.float32)
    key_rows = parts['key_rows'].astype(jnp.float32)
    grad_attn = jnp.einsum('qhd,khd->hqk', grad_mix, values)
    grad_values = jnp.einsum('hqk,qhd->khd', parts['attn'].astype(jnp.float32), grad_mix)
    grad_scores = rounded(jnp.where(parts['visible'], grad_attn * silu_slope(parts['scores']), 0.0)).astype(jnp.float32)
    grad_queries = jnp.einsum('hqk,khd->qhd', grad_scores, key_rows) * score_scale
    grad_keys = jnp.einsum('hqk,qhd->khd', grad_scores, queries) * score_scale
    grad_proj = jnp.concatenate([grad_gate, grad_values.reshape(length, width), grad_queries.reshape(length, width), grad_keys.reshape(length, width)], axis=1)
    grad_pre = rounded(grad_proj * silu_slope(parts['pre_act']))
    gw_proj = jnp.dot(parts['normed'].T, grad_pre, preferred_element_type=jnp.float32)
    grad_normed = jnp.dot(grad_pre, proj_weight.T, preferred_element_type=jnp.float32)
    grad_in = grad_out + norm_back(grad_normed, parts['normed_float'], parts['inverse_hidden'])
    return (grad_in, gw_proj, gw_out)

def reference(item_table, item_owner, item_row, staleness, w_proj, w_out, out_grad):
    ids = (item_owner[:, :, 0] * ROWS_OWN + item_row).astype(jnp.int32)
    item_rows = item_table[ids].astype(jnp.bfloat16)

    def one_user(totals, pieces):
        hidden, grad_last = pieces
        inputs = [hidden]
        for layer_index in range(LAYERS - 1):
            inputs.append(layer_forward(inputs[-1], w_proj[layer_index], w_out[layer_index]))
        gradient = grad_last.astype(jnp.float32)
        proj_list = []
        out_list = []
        for layer_index in reversed(range(LAYERS)):
            gradient, gw_proj, gw_out = layer_backward(inputs[layer_index], gradient, w_proj[layer_index], w_out[layer_index])
            proj_list.insert(0, gw_proj)
            out_list.insert(0, gw_out)
        new_totals = (totals[0] + jnp.stack(proj_list), totals[1] + jnp.stack(out_list))
        return (new_totals, gradient)
    start_totals = (jnp.zeros(w_proj.shape, jnp.float32), jnp.zeros(w_out.shape, jnp.float32))
    (proj_total, out_total), row_grad = lax.scan(one_user, start_totals, (item_rows, out_grad))
    table_grad = jnp.zeros(item_table.shape, jnp.float32).at[ids.reshape(-1)].add(row_grad.reshape(-1, D))
    step_rate = 0.5 / (1.0 + staleness.astype(jnp.float32))
    new_table = item_table - step_rate[:, None] * table_grad
    norm_scale = (N_FSDP * N_EMB * SEQ) ** (-0.5)
    return (new_table, proj_total * norm_scale, out_total * norm_scale)
```

```python
import jax
import jax.numpy as jnp
from jax import lax
from jax.experimental import pallas as pl
from jax.experimental.pallas import tpu as pltpu
from jax.sharding import PartitionSpec as P


DH = 64
F32 = jnp.float32
BF16 = jnp.bfloat16


def nt_dot(a, b):
    return lax.dot_general(a, b, (((1,), (1,)), ((), ())), preferred_element_type=F32)


def nn_dot(a, b):
    return jnp.dot(a, b, preferred_element_type=F32)


def index_kernel(owner_ref, row_ref, target_ref, request_ref):
    owners, capacity = request_ref.shape
    length = owner_ref.shape[1]
    lane = 128
    owner = owner_ref[...]
    member = (lax.broadcasted_iota(jnp.int32, (owners, length), 0) == owner).astype(F32)
    blocks = [member[:, at : at + lane] for at in range(0, length, lane)]
    stacked = jnp.concatenate(blocks, axis=0).astype(BF16)
    upper = (
        lax.broadcasted_iota(jnp.int32, (lane, lane), 0)
        < lax.broadcasted_iota(jnp.int32, (lane, lane), 1)
    ).astype(F32).astype(BF16)
    inside = nn_dot(stacked, upper)
    base = jnp.zeros((owners, 1), F32)
    slots = []
    for at, block in enumerate(blocks):
        earlier = inside[at * owners : (at + 1) * owners] + base
        slots.append(jnp.sum(earlier * block, axis=0, keepdims=True))
        base = base + jnp.sum(block, axis=1, keepdims=True)
    slot = jnp.concatenate(slots, axis=1).astype(jnp.int32)
    target_ref[...] = owner * capacity + slot
    value = row_ref[...] + 1
    high = (value >> 6).astype(F32)
    low = (value & 63).astype(F32)
    here = lax.broadcasted_iota(jnp.int32, (capacity, length), 0) == slot
    members = member.astype(BF16)
    high_of = nt_dot(members, jnp.where(here, high, 0.0).astype(BF16))
    low_of = nt_dot(members, jnp.where(here, low, 0.0).astype(BF16))
    request_ref[...] = (high_of * 64.0 + low_of).astype(jnp.int32) - 1


def slot_index(owner, offset, owners, capacity):
    length = owner.shape[1]
    return pl.pallas_call(
        index_kernel,
        out_shape=(
            jax.ShapeDtypeStruct((1, length), jnp.int32),
            jax.ShapeDtypeStruct((owners, capacity), jnp.int32),
        ),
        name="slot_index",
    )(owner, offset)


def lookup_kernel(request_ref, table_ref, out_ref):
    owners, capacity = request_ref.shape
    rows = table_ref.shape[0]
    asked = jnp.maximum(request_ref[...] + 1, 0)
    split = jnp.concatenate([(asked >> 6).astype(F32), (asked & 63).astype(F32)], axis=1)
    block = out_ref.shape[0]
    first = pl.program_id(0) * block
    slot_of = first + lax.broadcasted_iota(jnp.int32, (block, owners), 0)
    pick = (slot_of // capacity == lax.broadcasted_iota(jnp.int32, (block, owners), 1)).astype(F32)
    spread = nn_dot(pick.astype(BF16), split.astype(BF16))
    place = lax.rem(
        first + lax.broadcasted_iota(jnp.int32, (block, 2 * capacity), 0), capacity
    )
    lane_at = lax.rem(lax.broadcasted_iota(jnp.int32, (block, 2 * capacity), 1), capacity)
    spread = jnp.where(place == lane_at, spread, 0.0).astype(BF16)
    lanes = 128
    weight = jnp.where(
        lax.broadcasted_iota(jnp.int32, (2 * capacity, lanes), 0) < capacity, 64.0, 1.0
    ).astype(BF16)
    wanted = nn_dot(spread, weight).astype(jnp.int32) - 1
    total = jnp.zeros(out_ref.shape, F32)
    step = 512
    for at in range(0, rows, step):
        hot = [
            (wanted == at + part + lax.broadcasted_iota(jnp.int32, (block, lanes), 1))
            .astype(F32)
            .astype(BF16)
            for part in range(0, step, lanes)
        ]
        total = total + nn_dot(jnp.concatenate(hot, axis=1), table_ref[at : at + step])
    out_ref[...] = total.astype(BF16)


def look_up(requested, table):
    owners, capacity = requested.shape
    rows, width = table.shape
    slots = owners * capacity
    block = 256
    return pl.pallas_call(
        lookup_kernel,
        grid=(slots // block,),
        in_specs=[
            pl.BlockSpec((owners, capacity), lambda i: (0, 0)),
            pl.BlockSpec((rows, width), lambda i: (0, 0)),
        ],
        out_specs=pl.BlockSpec((block, width), lambda i: (i, 0)),
        out_shape=jax.ShapeDtypeStruct((slots, width), BF16),
        name="look_up",
    )(requested, table)


def place_kernel(target_ref, rows_ref, out_ref):
    length = target_ref.shape[0]
    slots = rows_ref.shape[0]
    hot = (lax.broadcasted_iota(jnp.int32, (length, slots), 1) == target_ref[...]).astype(F32)
    out_ref[...] = nn_dot(hot.astype(BF16), rows_ref[...]).astype(BF16)


def place_rows(target, rows):
    length = target.shape[0]
    slots, width = rows.shape
    block = 256
    return pl.pallas_call(
        place_kernel,
        grid=(length // block,),
        in_specs=[
            pl.BlockSpec((block, 1), lambda i: (i, 0)),
            pl.BlockSpec((slots, width), lambda i: (0, 0)),
        ],
        out_specs=pl.BlockSpec((block, width), lambda i: (i, 0)),
        out_shape=jax.ShapeDtypeStruct((length, width), BF16),
        name="place_rows",
    )(target, rows)


def send_kernel(target_ref, grad_ref, out_ref):
    block = out_ref.shape[0]
    length = grad_ref.shape[0]
    slot = pl.program_id(0) * block + lax.broadcasted_iota(jnp.int32, (block, length), 0)
    hot = (slot == target_ref[...]).astype(F32).astype(BF16)
    out_ref[...] = nn_dot(hot, grad_ref[...].astype(BF16)).astype(BF16)


def to_slots(target, gradient, slots):
    length, width = gradient.shape
    block = 256
    return pl.pallas_call(
        send_kernel,
        grid=(slots // block,),
        in_specs=[
            pl.BlockSpec((1, length), lambda i: (0, 0)),
            pl.BlockSpec((length, width), lambda i: (0, 0)),
        ],
        out_specs=pl.BlockSpec((block, width), lambda i: (i, 0)),
        out_shape=jax.ShapeDtypeStruct((slots, width), BF16),
        name="to_slots",
    )(target, gradient)


def update_kernel(request_ref, stale_ref, incoming_ref, table_ref, out_ref):
    block = out_ref.shape[0]
    slots = incoming_ref.shape[0]
    row = pl.program_id(0) * block + lax.broadcasted_iota(jnp.int32, (block, slots), 0)
    hot = (row == request_ref[...]).astype(F32).astype(BF16)
    table_grad = nn_dot(hot, incoming_ref[...])
    rate = 0.5 / (1.0 + stale_ref[...].astype(F32))
    out_ref[...] = table_ref[...] - rate * table_grad


def update_table(requested, staleness, incoming, table):
    rows, width = table.shape
    slots = incoming.shape[0]
    block = 512
    return pl.pallas_call(
        update_kernel,
        grid=(rows // block,),
        in_specs=[
            pl.BlockSpec((1, slots), lambda i: (0, 0)),
            pl.BlockSpec((block, 1), lambda i: (i, 0)),
            pl.BlockSpec((slots, width), lambda i: (0, 0)),
            pl.BlockSpec((block, width), lambda i: (i, 0)),
        ],
        out_specs=pl.BlockSpec((block, width), lambda i: (i, 0)),
        out_shape=jax.ShapeDtypeStruct((rows, width), F32),
        name="update_table",
    )(requested, staleness, incoming, table)


def swap(payload, axes):
    return lax.all_to_all(payload, axes, split_axis=0, concat_axis=0, tiled=True)


def gather_weights(w_proj, w_out):
    fsdp_count = lax.axis_size("fsdp")
    emb_count = lax.axis_size("emb")
    layers, rows, _ = w_proj.shape
    shard = jnp.concatenate([w_proj, w_out], axis=2).reshape(layers * rows, -1)
    piece = shard.shape[0] // emb_count
    mine = lax.dynamic_slice_in_dim(shard, lax.axis_index("emb") * piece, piece, 0)
    across = swap(jnp.broadcast_to(mine[None], (fsdp_count,) + mine.shape), "fsdp")
    every = swap(jnp.broadcast_to(across[None], (emb_count,) + across.shape), "emb")
    per = emb_count // layers
    whole = every.reshape(layers, per, fsdp_count, piece, -1).transpose(0, 2, 1, 3, 4)
    return whole.reshape(layers, fsdp_count * rows, -1)


def reduce_weights(grad, scale):
    fsdp_count = lax.axis_size("fsdp")
    emb_count = lax.axis_size("emb")
    rows, columns = grad.shape
    mine = rows // fsdp_count
    piece = mine // emb_count
    parts = grad.reshape(fsdp_count, emb_count, piece, columns).transpose(1, 0, 2, 3)
    plane = swap(parts.astype(BF16), "emb").astype(F32).sum(axis=0)
    total = swap(plane.astype(BF16), "fsdp").astype(F32).sum(axis=0) * scale
    total = total.astype(BF16)
    every = swap(jnp.broadcast_to(total[None], (emb_count,) + total.shape), "emb")
    return every.reshape(mine, columns).astype(F32)


EPSILON = 1e-05


def normalize(value):
    center = value - jnp.mean(value, axis=-1, keepdims=True)
    inverse = lax.rsqrt(jnp.mean(center * center, axis=-1, keepdims=True) + EPSILON)
    return (center * inverse, inverse)


def norm_back(gradient, normed, inverse):
    return inverse * (
        gradient
        - jnp.mean(gradient, axis=-1, keepdims=True)
        - normed * jnp.mean(gradient * normed, axis=-1, keepdims=True)
    )


def silu_slope(value):
    logistic = jax.nn.sigmoid(value)
    return logistic * (1.0 + value * (1.0 - logistic))


def causal(first_row, block_rows, length):
    query_pos = first_row + lax.broadcasted_iota(jnp.int32, (block_rows, length), 0)
    key_pos = lax.broadcasted_iota(jnp.int32, (block_rows, length), 1)
    return key_pos <= query_pos


def attend(queries, key_rows, values, block_rows, score_scale):
    length = queries.shape[0]
    results = []
    for block_index in range(length // block_rows):
        first_row = block_index * block_rows
        end_row = first_row + block_rows
        query_part = queries[first_row:end_row]
        scores = (
            jnp.einsum(
                "qhd,khd->hqk", query_part, key_rows[:end_row], preferred_element_type=jnp.float32
            )
            * score_scale
        )
        visible = causal(first_row, block_rows, end_row)[None]
        attn = jnp.where(visible, jax.nn.silu(scores), 0.0).astype(jnp.bfloat16)
        results.append(
            jnp.einsum("hqk,khd->qhd", attn, values[:end_row], preferred_element_type=jnp.float32)
        )
    mixture = jnp.concatenate(results, axis=0)
    return mixture.reshape(length, -1)


def attend_back(queries, key_rows, values, grad_mix, block_rows, score_scale):
    length = queries.shape[0]
    grad_keys = jnp.zeros(queries.shape, jnp.float32)
    grad_values = jnp.zeros(queries.shape, jnp.float32)
    query_grads = []
    for block_index in range(length // block_rows):
        first_row = block_index * block_rows
        end_row = first_row + block_rows
        query_part = queries[first_row:end_row]
        grad_part = grad_mix[first_row:end_row]
        key_part = key_rows[:end_row]
        value_part = values[:end_row]
        scores = (
            jnp.einsum("qhd,khd->hqk", query_part, key_part, preferred_element_type=jnp.float32)
            * score_scale
        )
        visible = causal(first_row, block_rows, end_row)[None]
        attn = jnp.where(visible, jax.nn.silu(scores), 0.0).astype(jnp.bfloat16)
        grad_attn = jnp.einsum(
            "qhd,khd->hqk", grad_part, value_part, preferred_element_type=jnp.float32
        )
        grad_values = grad_values.at[:end_row].add(
            jnp.einsum("hqk,qhd->khd", attn, grad_part, preferred_element_type=jnp.float32)
        )
        grad_scores = jnp.where(visible, grad_attn * silu_slope(scores), 0.0).astype(jnp.bfloat16)
        query_grads.append(
            jnp.einsum("hqk,khd->qhd", grad_scores, key_part, preferred_element_type=jnp.float32)
            * score_scale
        )
        grad_keys = grad_keys.at[:end_row].add(
            jnp.einsum("hqk,qhd->khd", grad_scores, query_part, preferred_element_type=jnp.float32)
            * score_scale
        )
    grad_queries = jnp.concatenate(query_grads, axis=0)
    return (
        grad_queries.reshape(length, -1),
        grad_keys.reshape(length, -1),
        grad_values.reshape(length, -1),
    )


def layer_parts(hidden, proj_weight, out_weight, block_rows):
    length = hidden.shape[0]
    width = out_weight.shape[0]
    head_count = width // DH
    hidden_float = hidden.astype(jnp.float32)
    normed_float, inverse_hidden = normalize(hidden_float)
    normed = normed_float.astype(jnp.bfloat16)
    pre_act = jnp.dot(normed, proj_weight, preferred_element_type=jnp.float32)
    projected = jax.nn.silu(pre_act).astype(jnp.bfloat16)
    gating = projected[:, :width]
    values = projected[:, width : 2 * width].reshape(length, head_count, DH)
    queries = projected[:, 2 * width : 3 * width].reshape(length, head_count, DH)
    key_rows = projected[:, 3 * width :].reshape(length, head_count, DH)
    mixture = attend(queries, key_rows, values, block_rows, DH ** (-0.5))
    mix_normed, inverse_mix = normalize(mixture)
    gated_out = (mix_normed * gating.astype(jnp.float32)).astype(jnp.bfloat16)
    return dict(
        hidden_float=hidden_float,
        normed_float=normed_float,
        inverse_hidden=inverse_hidden,
        normed=normed,
        pre_act=pre_act,
        gating=gating,
        values=values,
        queries=queries,
        key_rows=key_rows,
        mix_normed=mix_normed,
        inverse_mix=inverse_mix,
        gated_out=gated_out,
    )


def layer_forward(hidden, proj_weight, out_weight, block_rows):
    parts = layer_parts(hidden, proj_weight, out_weight, block_rows)
    branch = jnp.dot(parts["gated_out"], out_weight, preferred_element_type=jnp.float32)
    return ((parts["hidden_float"] + branch).astype(jnp.bfloat16), parts)


def layer_backward(hidden, grad_out, proj_weight, out_weight, block_rows, parts):
    if parts is None:
        parts = layer_parts(hidden, proj_weight, out_weight, block_rows)
    length = hidden.shape[0]
    width = out_weight.shape[0]
    grad_round = grad_out.astype(jnp.bfloat16)
    gw_out = jnp.dot(parts["gated_out"].T, grad_round, preferred_element_type=jnp.float32)
    grad_gated = jnp.dot(grad_round, out_weight.T, preferred_element_type=jnp.float32)
    grad_gate = grad_gated * parts["mix_normed"]
    grad_mixture = norm_back(
        grad_gated * parts["gating"].astype(jnp.float32), parts["mix_normed"], parts["inverse_mix"]
    )
    grad_mix = grad_mixture.astype(jnp.bfloat16).reshape(length, width // DH, DH)
    grad_queries, grad_keys, grad_values = attend_back(
        parts["queries"], parts["key_rows"], parts["values"], grad_mix, block_rows, DH ** (-0.5)
    )
    grad_proj = jnp.concatenate([grad_gate, grad_values, grad_queries, grad_keys], axis=1)
    grad_pre = (grad_proj * silu_slope(parts["pre_act"])).astype(jnp.bfloat16)
    gw_proj = jnp.dot(parts["normed"].T, grad_pre, preferred_element_type=jnp.float32)
    grad_normed = jnp.dot(grad_pre, proj_weight.T, preferred_element_type=jnp.float32)
    grad_in = grad_out + norm_back(grad_normed, parts["normed_float"], parts["inverse_hidden"])
    return (grad_in, gw_proj, gw_out)


def local(item_table, item_owner, item_row, staleness, w_proj, w_out, out_grad):
    fsdp_count = lax.axis_size("fsdp")
    emb_count = lax.axis_size("emb")
    owners = fsdp_count * emb_count
    length = item_row.shape[1]
    capacity = 2 * length // owners
    width = item_table.shape[1]
    layer_count = w_proj.shape[0]
    slots = owners * capacity
    both = ("fsdp", "emb")
    weights = gather_weights(w_proj, w_out)
    target, request = slot_index(item_owner.reshape(1, length), item_row, owners, capacity)
    requested = swap(request, both)
    looked_up = look_up(requested, item_table.astype(BF16))
    returned = swap(looked_up.reshape(owners, capacity, width), both).reshape(slots, width)
    item_rows = place_rows(target.reshape(length, 1), returned)
    inner = w_proj.shape[2]
    proj_all, out_all = weights[:, :, :inner], weights[:, :, inner:]
    block_rows = min(512, length)
    next_hidden, parts = layer_forward(item_rows, proj_all[0], out_all[0], block_rows)
    inputs = [item_rows, next_hidden]
    saved_parts = [parts, None]
    gradient = out_grad[0].astype(F32)
    norm_scale = (owners * length) ** (-0.5)
    proj_sums, out_sums = [], []
    for layer_index in reversed(range(layer_count)):
        gradient, gw_proj, gw_out = layer_backward(
            inputs[layer_index],
            gradient,
            proj_all[layer_index],
            out_all[layer_index],
            block_rows,
            saved_parts[layer_index],
        )
        total = reduce_weights(jnp.concatenate([gw_proj, gw_out], axis=1), norm_scale)
        proj_sums.insert(0, total[:, :inner])
        out_sums.insert(0, total[:, inner:])
    outgoing = to_slots(target, gradient, slots)
    incoming = swap(outgoing.reshape(owners, capacity, width), both).reshape(slots, width)
    new_table = update_table(
        requested.reshape(1, slots), staleness.reshape(-1, 1), incoming, item_table
    )
    return (new_table, jnp.stack(proj_sums), jnp.stack(out_sums))


def solution(mesh):
    return jax.shard_map(
        local,
        mesh=mesh,
        in_specs=(
            P(("fsdp", "emb"), None),
            P(("fsdp", "emb"), None, None),
            P(("fsdp", "emb"), None),
            P(("fsdp", "emb")),
            P(None, "fsdp", None),
            P(None, "fsdp", None),
            P(("fsdp", "emb"), None, None),
        ),
        out_specs=(P(("fsdp", "emb"), None), P(None, "fsdp", None), P(None, "fsdp", None)),
        check_vma=False,
    )
```

```python
import functools

import jax
import jax.numpy as jnp
from jax import lax
from jax.experimental import pallas as pl
from jax.experimental.pallas import tpu as pltpu
from jax.sharding import PartitionSpec as P

DH = 64
EPSILON = 1e-05
F32 = jnp.float32
BF16 = jnp.bfloat16


def nt_dot(a, b):
    return lax.dot_general(a, b, (((1,), (1,)), ((), ())), preferred_element_type=F32)


def nn_dot(a, b):
    return jnp.dot(a, b, preferred_element_type=F32)


def as_column(row):
    side = row.shape[1]
    same = lax.broadcasted_iota(jnp.int32, (side, side), 0) == lax.broadcasted_iota(
        jnp.int32, (side, side), 1
    )
    return jnp.sum(jnp.where(same, row.astype(F32), 0.0), axis=1, keepdims=True)


def index_kernel(owner_ref, row_ref, target_ref, request_ref):
    owners, capacity = request_ref.shape
    length = owner_ref.shape[1]
    lane = 128
    owner = owner_ref[...]
    member = (lax.broadcasted_iota(jnp.int32, (owners, length), 0) == owner).astype(F32)
    blocks = [member[:, at : at + lane] for at in range(0, length, lane)]
    stacked = jnp.concatenate(blocks, axis=0).astype(BF16)
    upper = (
        lax.broadcasted_iota(jnp.int32, (lane, lane), 0)
        < lax.broadcasted_iota(jnp.int32, (lane, lane), 1)
    ).astype(F32).astype(BF16)
    inside = nn_dot(stacked, upper)
    base = jnp.zeros((owners, 1), F32)
    slots = []
    for at, block in enumerate(blocks):
        earlier = inside[at * owners : (at + 1) * owners] + base
        slots.append(jnp.sum(earlier * block, axis=0, keepdims=True))
        base = base + jnp.sum(block, axis=1, keepdims=True)
    slot = jnp.concatenate(slots, axis=1).astype(jnp.int32)
    target_ref[...] = owner * capacity + slot
    value = row_ref[...] + 1
    high = (value >> 6).astype(F32)
    low = (value & 63).astype(F32)
    here = lax.broadcasted_iota(jnp.int32, (capacity, length), 0) == slot
    members = member.astype(BF16)
    high_of = nt_dot(members, jnp.where(here, high, 0.0).astype(BF16))
    low_of = nt_dot(members, jnp.where(here, low, 0.0).astype(BF16))
    request_ref[...] = (high_of * 64.0 + low_of).astype(jnp.int32) - 1


def slot_index(owner, offset, owners, capacity):
    length = owner.shape[1]
    return pl.pallas_call(
        index_kernel,
        out_shape=(
            jax.ShapeDtypeStruct((1, length), jnp.int32),
            jax.ShapeDtypeStruct((owners, capacity), jnp.int32),
        ),
        compiler_params=pltpu.CompilerParams(vmem_limit_bytes=8 << 20),
        name="slot_index",
    )(owner, offset)


def lookup_kernel(request_ref, table_ref, out_ref, low_ref, high_ref, total_ref):
    owners, capacity = request_ref.shape
    slots = owners * capacity
    lanes = 128
    step, steps = pl.program_id(0), pl.num_programs(0)
    some = table_ref.shape[0]

    @pl.when(step == 0)
    def _():
        asked = jnp.maximum(request_ref[...] + 1, 0)
        split = jnp.concatenate([(asked >> 6).astype(F32), (asked & 63).astype(F32)], axis=1)
        weight = jnp.where(
            lax.broadcasted_iota(jnp.int32, (2 * capacity, lanes), 0) < capacity, 64.0, 1.0
        ).astype(BF16)
        block = 256

        def expand(index, carry):
            first = index * block
            slot_of = first + lax.broadcasted_iota(jnp.int32, (block, owners), 0)
            owner_at = lax.broadcasted_iota(jnp.int32, (block, owners), 1)
            pick = (slot_of // capacity == owner_at).astype(F32)
            spread = nn_dot(pick.astype(BF16), split.astype(BF16))
            place_at = lax.rem(
                first + lax.broadcasted_iota(jnp.int32, (block, 2 * capacity), 0), capacity
            )
            lane_at = lax.rem(lax.broadcasted_iota(jnp.int32, (block, 2 * capacity), 1), capacity)
            spread = jnp.where(place_at == lane_at, spread, 0.0).astype(BF16)
            wanted = nn_dot(spread, weight).astype(jnp.int32) - 1
            lane_row = lax.broadcasted_iota(jnp.int32, (block, lanes), 1)
            rows = rows_at(index, block)
            high_ref[rows] = (wanted >> 7).astype(F32).astype(BF16)
            low_ref[rows] = ((wanted & (lanes - 1)) == lane_row).astype(F32).astype(BF16)
            return carry

        lax.fori_loop(0, slots // block, expand, 0)

    low, high = low_ref[...], high_ref[...]
    none = jnp.zeros_like(low)
    first = step * (some // lanes)
    hot = [
        jnp.where(high == (first + at).astype(F32).astype(BF16), low, none)
        for at in range(some // lanes)
    ]
    part = nn_dot(jnp.concatenate(hot, axis=1), table_ref[...].astype(BF16))

    @pl.when(step == 0)
    def _():
        total_ref[...] = part

    @pl.when((step > 0) & (step < steps - 1))
    def _():
        total_ref[...] += part

    @pl.when(step == steps - 1)
    def _():
        out_ref[...] = (total_ref[...] + part).astype(BF16)


def look_up(requested, table):
    owners, capacity = requested.shape
    rows, width = table.shape
    slots = owners * capacity
    some = rows // 4
    return pl.pallas_call(
        lookup_kernel,
        grid=(rows // some,),
        in_specs=[
            pl.BlockSpec((owners, capacity), lambda i: (0, 0)),
            pl.BlockSpec((some, width), lambda i: (i, 0)),
        ],
        out_specs=pl.BlockSpec((slots, width), lambda i: (0, 0)),
        out_shape=jax.ShapeDtypeStruct((slots, width), BF16),
        scratch_shapes=[
            pltpu.VMEM((slots, 128), BF16),
            pltpu.VMEM((slots, 128), BF16),
            pltpu.VMEM((slots, width), F32),
        ],
        compiler_params=pltpu.CompilerParams(vmem_limit_bytes=62 << 20),
        name="look_up",
    )(requested, table)


def update_kernel(request_ref, stale_ref, incoming_ref, table_ref, out_ref, low_ref, high_ref):
    block = out_ref.shape[0]
    group, slots = low_ref.shape

    @pl.when(pl.program_id(0) == 0)
    def _():
        asked = request_ref[...]
        row = lax.broadcasted_iota(jnp.int32, (group, slots), 0)
        low_ref[...] = ((asked & (group - 1)) == row).astype(F32).astype(BF16)
        high_ref[...] = jnp.broadcast_to((asked >> (group.bit_length() - 1)).astype(F32), high_ref.shape).astype(BF16)

    low = low_ref[...]
    high = jnp.concatenate([high_ref[...]] * (group // high_ref.shape[0]), axis=0)
    none = jnp.zeros_like(low)
    first = pl.program_id(0) * (block // group)
    hot = [
        jnp.where(high == (first + at).astype(F32).astype(BF16), low, none)
        for at in range(block // group)
    ]
    table_grad = nn_dot(jnp.concatenate(hot, axis=0), incoming_ref[...])
    stale = [as_column(stale_ref[0, at : at + 1, :]) for at in range(stale_ref.shape[1])]
    rate = 0.5 / (1.0 + jnp.concatenate(stale, axis=0))
    out_ref[...] = table_ref[...] - rate * table_grad


def update_table(requested, staleness, incoming, table):
    rows, width = table.shape
    slots = incoming.shape[0]
    block, group = 1024, 256
    return pl.pallas_call(
        update_kernel,
        grid=(rows // block,),
        in_specs=[
            pl.BlockSpec((1, slots), lambda i: (0, 0)),
            pl.BlockSpec((1, block // 128, 128), lambda i: (i, 0, 0)),
            pl.BlockSpec((slots, width), lambda i: (0, 0)),
            pl.BlockSpec((block, width), lambda i: (i, 0)),
        ],
        out_specs=pl.BlockSpec((block, width), lambda i: (i, 0)),
        out_shape=jax.ShapeDtypeStruct((rows, width), F32),
        scratch_shapes=[pltpu.VMEM((group, slots), BF16), pltpu.VMEM((16, slots), BF16)],
        compiler_params=pltpu.CompilerParams(vmem_limit_bytes=32 << 20),
        name="update_table",
    )(requested, staleness.reshape(rows // block, block // 128, 128), incoming, table)


def swap(payload, axes):
    return lax.all_to_all(payload, axes, split_axis=0, concat_axis=0, tiled=True)


def axis_bits(name):
    size = lax.axis_size(name)
    return [1 << bit for bit in range(size.bit_length() - 1)]


def trade(payload, name, flip):
    size = lax.axis_size(name)
    return lax.ppermute(payload, name, [(at, at ^ flip) for at in range(size)])


def spread_plane(piece):
    whole = piece[None]
    for bit in reversed(axis_bits("emb")):
        other = trade(whole, "emb", bit)
        upper = (lax.axis_index("emb") & bit) != 0
        first = jnp.where(upper, other, whole)
        second = jnp.where(upper, whole, other)
        whole = jnp.stack([first, second], axis=1).reshape((-1,) + piece.shape)
    return whole


def reorder_bits(whole):
    bits = len(axis_bits("emb"))
    cube = whole.reshape((2,) * bits + whole.shape[1:])
    order = tuple(reversed(range(bits))) + tuple(range(bits, cube.ndim))
    return cube.transpose(order).reshape(whole.shape)


def gather_weights(w_proj, w_out):
    fsdp_count = lax.axis_size("fsdp")
    emb_count = lax.axis_size("emb")
    layers, rows, _ = w_proj.shape
    piece = layers * rows // emb_count
    first = lax.axis_index("emb") * piece
    mine = jnp.concatenate(
        [
            lax.dynamic_slice_in_dim(shard.reshape(layers * rows, -1), first, piece, 0)
            for shard in (w_proj, w_out)
        ],
        axis=1,
    )
    taken = [mine] + [trade(mine, "fsdp", flip) for flip in range(1, fsdp_count)]
    index = lax.axis_index("fsdp")
    across = []
    for want in range(fsdp_count):
        chosen = taken[0]
        for flip in range(1, fsdp_count):
            chosen = jnp.where((index ^ flip) == want, taken[flip], chosen)
        across.append(chosen)
    every = spread_plane(jnp.stack(across))
    per = emb_count // layers
    whole = every.reshape(layers, per, fsdp_count, piece, -1).transpose(0, 2, 1, 3, 4)
    return whole.reshape(layers, fsdp_count * rows, -1)


def weight_pieces(gw_proj, gw_out):
    if len(gw_proj.shape) == 4:
        return gw_proj
    fsdp_count = lax.axis_size("fsdp")
    emb_count = lax.axis_size("emb")
    rows = gw_proj.shape[0] // fsdp_count
    cols = gw_proj.shape[1] // emb_count
    proj = gw_proj.reshape(fsdp_count, rows, emb_count, cols).transpose(2, 0, 1, 3)
    out = gw_out.reshape(fsdp_count, emb_count, rows // emb_count, -1, cols)
    out = out.transpose(1, 0, 3, 2, 4).reshape(emb_count, fsdp_count, -1, cols)
    return jnp.concatenate([proj, out], axis=2)


def plane_sum_whole(pieces):
    return swap(pieces, "emb").astype(F32).sum(axis=0)


def plane_sum_halving(pieces, ordered):
    bits = axis_bits("emb")
    held = pieces if ordered else reorder_bits(pieces)
    for bit in bits:
        half = held.shape[0] // 2
        upper = (lax.axis_index("emb") & bit) != 0
        low, high = held[:half], held[half:]
        got = trade(jnp.where(upper, low, high).astype(BF16), "emb", bit)
        held = jnp.where(upper, high, low).astype(F32) + got.astype(F32)
    return held[0]


def finish_weights(planes, scale):
    fsdp_count = lax.axis_size("fsdp")
    index = lax.axis_index("fsdp")
    held = planes.astype(BF16)
    total = lax.dynamic_index_in_dim(planes, index, 0, keepdims=False)
    for flip in range(1, fsdp_count):
        leaving = lax.dynamic_index_in_dim(held, index ^ flip, 0, keepdims=False)
        total = total + trade(leaving, "fsdp", flip).astype(F32)
    return spread_plane((total * scale).astype(BF16))


def unpack_weights(every, rows, width):
    emb_count = every.shape[0]
    proj = every[:, :rows].transpose(1, 0, 2).reshape(rows, -1)
    out = every[:, rows:].reshape(emb_count, -1, rows // emb_count, every.shape[2])
    out = out.transpose(0, 2, 1, 3).reshape(rows, width)
    return proj.astype(F32), out.astype(F32)


BLOCK = 256


def normalize(value):
    center = value - jnp.mean(value, axis=-1, keepdims=True)
    inverse = lax.rsqrt(jnp.mean(center * center, axis=-1, keepdims=True) + EPSILON)
    return center * inverse, inverse


def norm_back(gradient, normed, inverse):
    return inverse * (
        gradient
        - jnp.mean(gradient, axis=-1, keepdims=True)
        - normed * jnp.mean(gradient * normed, axis=-1, keepdims=True)
    )


def silu_slope(value):
    half = 0.5 * value
    turn = jnp.tanh(half)
    grown = 1.0 + turn
    return 0.5 * (grown + half * grown * (1.0 - turn))


def rows_at(index, size=BLOCK):
    return pl.ds(pl.multiple_of(index * size, size), size)


def head_masks(width):
    lane = lax.broadcasted_iota(jnp.int32, (1, width), 1) // DH
    return [(lane == head).astype(F32).astype(BF16) for head in range(width // DH)]


def fill_stack(ref, index, value, masks):
    for head, mask in enumerate(masks):
        ref[index, head * BLOCK : (head + 1) * BLOCK, :] = value * mask


def project(hidden_ref, weight, bufs, masks, keep):
    width = hidden_ref.shape[1]
    unit = 0.5 * DH ** (-0.5)

    def step(index, carry):
        rows = rows_at(index)
        normed, _ = normalize(hidden_ref[rows].astype(F32))
        normed = normed.astype(BF16)
        pre = nn_dot(normed, weight[:, : 4 * width])
        if keep:
            bufs["pre"][rows] = pre
            bufs["normed"][:, rows] = normed.astype(F32).T.astype(BF16)
        half = 0.5 * pre
        out = (half + half * jnp.tanh(half)).astype(BF16)
        values = out[:, width : 2 * width]
        queries = out[:, 2 * width : 3 * width] * BF16(unit)
        keys = out[:, 3 * width :]
        bufs["gate"][rows] = out[:, :width]
        bufs["keys"][rows] = keys
        bufs["queries"][rows] = queries
        fill_stack(bufs["q_stack"], index, queries, masks)
        fill_stack(bufs["v_stack"], index, values, masks)
        if keep:
            fill_stack(bufs["k_stack"], index, keys, masks)
            bufs["keys_t"][:, rows] = ((keys * BF16(unit)).astype(F32).T).astype(BF16)
        return carry

    lax.fori_loop(0, hidden_ref.shape[0] // BLOCK, step, 0)


def attend(mix_ref, bufs, heads):
    blocks = mix_ref.shape[0] // BLOCK
    ahead = lax.broadcasted_iota(jnp.int32, (BLOCK, BLOCK), 1) - lax.broadcasted_iota(
        jnp.int32, (BLOCK, BLOCK), 0
    )

    def query_step(at, carry):
        rows = rows_at(at)

        def key_step(to, total):
            keys = bufs["keys"][rows_at(to)]
            visible = ahead <= (at - to) * BLOCK
            parts = []
            for head in range(heads):
                lifted = bufs["q_stack"][at, head * BLOCK : (head + 1) * BLOCK, :]
                half = nt_dot(lifted, keys)
                attn = half + half * jnp.tanh(half)
                parts.append(jnp.where(visible, attn, 0.0).astype(BF16))
            return total + nn_dot(jnp.concatenate(parts, axis=1), bufs["v_stack"][to])

        mix_ref[rows] = lax.fori_loop(
            0, at + 1, key_step, jnp.zeros((BLOCK, mix_ref.shape[1]), F32)
        )
        return carry

    lax.fori_loop(0, blocks, query_step, 0)


def finish_forward(hidden_ref, mix_ref, weight, gate_ref, next_ref):
    width = hidden_ref.shape[1]

    def step(index, carry):
        rows = rows_at(index)
        mixed, _ = normalize(mix_ref[rows])
        gated = (mixed * gate_ref[rows].astype(F32)).astype(BF16)
        branch = nn_dot(gated, weight[:, 4 * width :])
        next_ref[rows] = (hidden_ref[rows].astype(F32) + branch).astype(BF16)
        return carry

    lax.fori_loop(0, hidden_ref.shape[0] // BLOCK, step, 0)


def backward(hidden_ref, grad_in, grad_out, weight, mix_ref, gw_proj_ref, gw_out_ref, bufs, masks, flip):
    length, width = hidden_ref.shape
    heads = len(masks)
    blocks = length // BLOCK
    pre_ref, gpre_ref, gm_ref = bufs["pre"], bufs["gpre"], bufs["gm"]

    def enter(index, carry):
        rows = rows_at(index)
        gradient = grad_in[rows].astype(BF16)
        mixed, inverse = normalize(mix_ref[rows])
        gate = bufs["gate"][rows].astype(F32)
        gated = mixed * gate
        bufs["gated"][:, rows] = gated.T.astype(BF16)
        grad_gated = nt_dot(gradient, weight[:, 4 * width :])
        slope = silu_slope(pre_ref[rows, :width])
        gpre_ref[rows, :width] = (grad_gated * mixed * slope).astype(BF16)
        grad_mix = norm_back(grad_gated * gate, mixed, inverse).astype(BF16)
        gm_ref[rows] = grad_mix
        fill_stack(bufs["g_stack"], index, grad_mix, masks)
        bufs["gq"][:, rows] = jnp.zeros((width, BLOCK), F32)
        bufs["round"][rows] = gradient
        return carry

    lax.fori_loop(0, blocks, enter, 0)
    store_out_pieces(gw_out_ref, gw_proj_ref, nn_dot(bufs["gated"][...], bufs["round"][...]), flip)
    ahead = lax.broadcasted_iota(jnp.int32, (BLOCK, BLOCK), 0) - lax.broadcasted_iota(
        jnp.int32, (BLOCK, BLOCK), 1
    )

    def key_step(to, carry):
        keys_at = rows_at(to)

        def query_step(at, totals):
            grad_values, grad_keys = totals
            cols = rows_at(at)
            queries = bufs["queries"][cols]
            grad_mix = gm_ref[cols]
            visible = ahead <= (at - to) * BLOCK
            attns, grads = [], []
            halves = nt_dot(bufs["k_stack"][to], queries)
            grad_attns = nt_dot(bufs["v_stack"][to], grad_mix)
            for head in range(heads):
                span = slice(head * BLOCK, (head + 1) * BLOCK)
                half = halves[span]
                grad_attn = grad_attns[span]
                turn = jnp.tanh(half)
                grown = 1.0 + turn
                attn = half * grown
                slope = grown + attn * (1.0 - turn)
                attns.append(jnp.where(visible, attn, 0.0).astype(BF16))
                grad_score = jnp.where(visible, grad_attn * slope, 0.0).astype(BF16)
                grads.append(grad_score)
                place = slice(head * DH, (head + 1) * DH)
                bufs["gq"][place, cols] += nn_dot(bufs["keys_t"][place, keys_at], grad_score)
            grad_values += nn_dot(jnp.concatenate(attns, axis=1), bufs["g_stack"][at])
            grad_keys += nn_dot(jnp.concatenate(grads, axis=1), bufs["q_stack"][at])
            return grad_values, grad_keys

        zero = jnp.zeros((BLOCK, width), F32)
        grad_values, grad_keys = lax.fori_loop(to, blocks, query_step, (zero, zero))
        slope = silu_slope(pre_ref[keys_at, width : 2 * width])
        gpre_ref[keys_at, width : 2 * width] = (grad_values * slope).astype(BF16)
        slope = silu_slope(pre_ref[keys_at, 3 * width :])
        gpre_ref[keys_at, 3 * width :] = (grad_keys * slope).astype(BF16)
        return carry

    lax.fori_loop(0, blocks, key_step, 0)

    def leave(index, carry):
        rows = rows_at(index)
        slope = silu_slope(pre_ref[rows, 2 * width : 3 * width])
        gpre_ref[rows, 2 * width : 3 * width] = (bufs["gq"][:, rows].T * slope).astype(BF16)
        grad_normed = nt_dot(gpre_ref[rows, :], weight[:, : 4 * width])
        normed, inverse = normalize(hidden_ref[rows].astype(F32))
        gradient = grad_in[rows].astype(F32) + norm_back(grad_normed, normed, inverse)
        grad_out[rows] = gradient.astype(grad_out.dtype)
        return carry

    lax.fori_loop(0, blocks, leave, 0)

    def weigh(index, carry):
        cols = rows_at(index)
        grad = nn_dot(bufs["normed"][...], gpre_ref[:, cols]).astype(BF16)
        if len(gw_proj_ref.shape) == 2:
            gw_proj_ref[:, cols] = grad
            return carry
        peers, shards, _, lanes = gw_proj_ref.shape
        deep = width // shards
        for part in range(BLOCK // lanes):
            for shard in range(shards):
                gw_proj_ref[turn_bits(index * (BLOCK // lanes) + part, peers, flip), shard, :deep, :] = grad[
                    shard * deep : (shard + 1) * deep, part * lanes : (part + 1) * lanes
                ]
        return carry

    lax.fori_loop(0, 4 * width // BLOCK, weigh, 0)


def turn_bits(index, count, flip):
    if not flip:
        return index
    bits = count.bit_length() - 1
    return sum(((index >> bit) & 1) << (bits - 1 - bit) for bit in range(bits))


def store_out_pieces(gw_out_ref, gw_proj_ref, grad, flip):
    if len(gw_proj_ref.shape) == 2:
        gw_out_ref[...] = grad.astype(BF16)
        return
    peers, shards, rows, lanes = gw_proj_ref.shape
    width = grad.shape[0]
    deep = width // shards
    some = deep // peers
    for shard in range(shards):
        for peer in range(peers):
            first = shard * deep + peer * some
            piece = [
                grad[first : first + some, at : at + lanes] for at in range(0, width, lanes)
            ]
            gw_proj_ref[turn_bits(peer, peers, flip), shard, deep:rows, :] = jnp.concatenate(piece, axis=0).astype(BF16)
    gw_out_ref[...] = jnp.zeros(gw_out_ref.shape, BF16)


def weight_shapes(width, shards, peers):
    deep = width // shards
    lanes = 4 * width // peers
    if lanes == 128 and deep // peers == 8 and deep % 16 == 0:
        rows = deep + deep // peers * width // lanes
        return [
            jax.ShapeDtypeStruct((peers, shards, rows, lanes), BF16),
            jax.ShapeDtypeStruct((8, 128), BF16),
        ]
    return [
        jax.ShapeDtypeStruct((width, 4 * width), BF16),
        jax.ShapeDtypeStruct((width, width), BF16),
    ]


def layer_buffers(length, width):
    heads = width // DH
    blocks = length // BLOCK
    stack = pltpu.VMEM((blocks, heads * BLOCK, width), BF16)
    plain = pltpu.VMEM((length, width), BF16)
    turned = pltpu.VMEM((width, length), BF16)
    return dict(
        pre=pltpu.VMEM((length, 4 * width), F32),
        gpre=pltpu.VMEM((length, 4 * width), BF16),
        normed=turned,
        gated=turned,
        keys_t=turned,
        gq=pltpu.VMEM((width, length), F32),
        gate=plain,
        keys=plain,
        queries=plain,
        gm=plain,
        round=plain,
        q_stack=stack,
        k_stack=stack,
        v_stack=stack,
        g_stack=stack,
    )


def top_kernel(names, layers, target_ref, rows_ref, weights_ref, cot_ref, *refs):
    hidden_refs, refs = refs[:layers], refs[layers:]
    mix_refs, refs = refs[: layers - 1], refs[layers - 1 :]
    grad_ref, gw_proj_ref, gw_out_ref, last_mix_ref = refs[:4]
    bufs = dict(zip(names, refs[4:]))
    width = rows_ref.shape[1]
    masks = head_masks(width)
    place(target_ref, rows_ref, hidden_refs[0])
    for layer in range(layers):
        last = layer == layers - 1
        weight = weights_ref.at[layer]
        mix_ref = last_mix_ref if last else mix_refs[layer]
        project(hidden_refs[layer], weight, bufs, masks, last)
        attend(mix_ref, bufs, len(masks))
        if not last:
            finish_forward(
                hidden_refs[layer], mix_ref, weight, bufs["gate"], hidden_refs[layer + 1]
            )
    backward(
        hidden_refs[-1],
        cot_ref,
        grad_ref,
        weights_ref.at[layers - 1],
        last_mix_ref,
        gw_proj_ref,
        gw_out_ref,
        bufs,
        masks,
        False,
    )


def place(target_ref, rows_ref, out_ref):
    slots = rows_ref.shape[0]

    def step(index, carry):
        rows = rows_at(index)
        wanted = jnp.concatenate(
            [
                as_column(target_ref[:, pl.ds(pl.multiple_of(index * BLOCK + at, 128), 128)])
                for at in range(0, BLOCK, 128)
            ],
            axis=0,
        )
        wanted = jnp.broadcast_to(wanted.astype(jnp.int32), (BLOCK, 128))
        high = (wanted >> 7).astype(F32).astype(BF16)
        lane_row = lax.broadcasted_iota(jnp.int32, (BLOCK, 128), 1)
        low = ((wanted & 127) == lane_row).astype(F32).astype(BF16)
        none = jnp.zeros_like(low)
        hot = [jnp.where(high == BF16(at), low, none) for at in range(slots // 128)]
        out_ref[rows] = nn_dot(jnp.concatenate(hot, axis=1), rows_ref[...]).astype(BF16)
        return carry

    lax.fori_loop(0, out_ref.shape[0] // BLOCK, step, 0)


def run_top(target, rows, weights, cotangent, shards, peers):
    layers = weights.shape[0]
    length, width = cotangent.shape
    buffers = layer_buffers(length, width)
    hidden = jax.ShapeDtypeStruct((length, width), BF16)
    wide = jax.ShapeDtypeStruct((length, width), F32)
    return pl.pallas_call(
        functools.partial(top_kernel, tuple(buffers), layers),
        out_shape=[hidden] * layers
        + [wide] * (layers - 1)
        + [wide]
        + weight_shapes(width, shards, peers),
        scratch_shapes=[pltpu.VMEM((length, width), F32)] + list(buffers.values()),
        compiler_params=pltpu.CompilerParams(vmem_limit_bytes=44 << 20),
        name="forward_and_last_backward",
    )(target, rows, weights, cotangent)


def lower_kernel(
    names, layer, target_ref, hidden_ref, mix_ref, weights_ref, grad_ref, out_ref, gw_proj_ref, gw_out_ref, done_ref, *refs
):
    bufs = dict(zip(names, refs))
    masks = head_masks(hidden_ref.shape[1])
    weight = weights_ref.at[layer]
    project(hidden_ref, weight, bufs, masks, True)
    first = layer == 0
    backward(
        hidden_ref,
        grad_ref,
        done_ref if first else out_ref,
        weight,
        mix_ref,
        gw_proj_ref,
        gw_out_ref,
        bufs,
        masks,
        True,
    )
    if not first:
        return
    length = hidden_ref.shape[0]

    target = jnp.broadcast_to(target_ref[...], (BLOCK, length))
    slot_row = lax.broadcasted_iota(jnp.int32, (BLOCK, length), 0)
    low = ((target & (BLOCK - 1)) == slot_row).astype(F32).astype(BF16)
    high = (target >> (BLOCK.bit_length() - 1)).astype(F32).astype(BF16)
    none = jnp.zeros_like(low)
    group = 4 * BLOCK

    def send(index, carry):
        hot = [
            jnp.where(high == (4 * index + at).astype(F32).astype(BF16), low, none)
            for at in range(4)
        ]
        out_ref[rows_at(index, group)] = nn_dot(
            jnp.concatenate(hot, axis=0), done_ref[...]
        ).astype(BF16)
        return carry

    lax.fori_loop(0, out_ref.shape[0] // group, send, 0)


def run_lower(layer, target, hidden, mix, weights, gradient, slots, shards, peers):
    length, width = hidden.shape
    buffers = layer_buffers(length, width)
    result = (
        jax.ShapeDtypeStruct((slots, width), BF16)
        if layer == 0
        else jax.ShapeDtypeStruct((length, width), F32)
    )
    return pl.pallas_call(
        functools.partial(lower_kernel, tuple(buffers), layer),
        out_shape=[result] + weight_shapes(width, shards, peers),
        scratch_shapes=[pltpu.VMEM((length, width), BF16)] + list(buffers.values()),
        compiler_params=pltpu.CompilerParams(vmem_limit_bytes=44 << 20),
        name="lower_backward",
    )(target, hidden, mix, weights, gradient)


def local(item_table, item_owner, item_row, staleness, w_proj, w_out, out_grad):
    fsdp_count = lax.axis_size("fsdp")
    emb_count = lax.axis_size("emb")
    owners = fsdp_count * emb_count
    length = item_row.shape[1]
    capacity = 2 * length // owners
    width = item_table.shape[1]
    layer_count, shard_rows, _ = w_proj.shape
    slots = owners * capacity
    both = ("fsdp", "emb")
    weights = gather_weights(w_proj, w_out)
    target, request = slot_index(item_owner.reshape(1, length), item_row, owners, capacity)
    requested = swap(request, both)
    looked_up = look_up(requested, item_table)
    returned = swap(looked_up.reshape(owners, capacity, width), both)
    returned, asked = lax.optimization_barrier(
        (returned.reshape(slots, width), requested.reshape(1, slots))
    )
    norm_scale = (owners * length) ** (-0.5)
    outs = run_top(target, returned, weights, out_grad[0], fsdp_count, emb_count)
    hiddens, mixes = outs[:layer_count], outs[layer_count : 2 * layer_count - 1]
    gradient, gw_proj, gw_out = outs[2 * layer_count - 1 :]
    planes = [plane_sum_whole(weight_pieces(gw_proj, gw_out))]
    for layer in reversed(range(layer_count - 1)):
        gradient, gw_proj, gw_out = run_lower(
            layer,
            target,
            hiddens[layer],
            mixes[layer],
            weights,
            gradient,
            slots,
            fsdp_count,
            emb_count,
        )
        pieces = weight_pieces(gw_proj, gw_out)
        planes.insert(0, plane_sum_halving(pieces, len(gw_proj.shape) == 4))
    incoming = swap(gradient.reshape(owners, capacity, width), both)
    incoming = incoming.reshape(slots, width)
    new_table = update_table(asked, staleness, incoming, item_table)
    every = finish_weights(jnp.stack(planes, axis=1), norm_scale)
    sums = [unpack_weights(every[:, at], shard_rows, width) for at in range(layer_count)]
    return (
        new_table,
        jnp.stack([proj for proj, _ in sums]),
        jnp.stack([out for _, out in sums]),
    )


def solution(mesh):
    return jax.shard_map(
        local,
        mesh=mesh,
        in_specs=(
            P(("fsdp", "emb"), None),
            P(("fsdp", "emb"), None, None),
            P(("fsdp", "emb"), None),
            P(("fsdp", "emb")),
            P(None, "fsdp", None),
            P(None, "fsdp", None),
            P(("fsdp", "emb"), None, None),
        ),
        out_specs=(P(("fsdp", "emb"), None), P(None, "fsdp", None), P(None, "fsdp", None)),
        check_vma=False,
    )
```

```python
import functools

import jax
import jax.numpy as jnp
from jax import lax
from jax.experimental import pallas as pl
from jax.experimental.pallas import tpu as pltpu
from jax.sharding import PartitionSpec as P

DH = 64
EPSILON = 1e-05
F32 = jnp.float32
BF16 = jnp.bfloat16


def nt_dot(a, b):
    return lax.dot_general(a, b, (((1,), (1,)), ((), ())), preferred_element_type=F32)


def nn_dot(a, b):
    return jnp.dot(a, b, preferred_element_type=F32)


def as_column(row):
    side = row.shape[1]
    same = lax.broadcasted_iota(jnp.int32, (side, side), 0) == lax.broadcasted_iota(
        jnp.int32, (side, side), 1
    )
    return jnp.sum(jnp.where(same, row.astype(F32), 0.0), axis=1, keepdims=True)


def index_kernel(owner_ref, row_ref, target_ref, request_ref):
    owners, capacity = request_ref.shape
    length = owner_ref.shape[1]
    lane = 128
    owner = owner_ref[...]
    member = (lax.broadcasted_iota(jnp.int32, (owners, length), 0) == owner).astype(F32)
    blocks = [member[:, at : at + lane] for at in range(0, length, lane)]
    stacked = jnp.concatenate(blocks, axis=0).astype(BF16)
    upper = (
        lax.broadcasted_iota(jnp.int32, (lane, lane), 0)
        < lax.broadcasted_iota(jnp.int32, (lane, lane), 1)
    ).astype(F32).astype(BF16)
    inside = nn_dot(stacked, upper)
    base = jnp.zeros((owners, 1), F32)
    slots = []
    for at, block in enumerate(blocks):
        earlier = inside[at * owners : (at + 1) * owners] + base
        slots.append(jnp.sum(earlier * block, axis=0, keepdims=True))
        base = base + jnp.sum(block, axis=1, keepdims=True)
    slot = jnp.concatenate(slots, axis=1).astype(jnp.int32)
    target_ref[...] = owner * capacity + slot
    value = row_ref[...] + 1
    high = (value >> 6).astype(F32)
    low = (value & 63).astype(F32)
    here = lax.broadcasted_iota(jnp.int32, (capacity, length), 0) == slot
    members = member.astype(BF16)
    high_of = nt_dot(members, jnp.where(here, high, 0.0).astype(BF16))
    low_of = nt_dot(members, jnp.where(here, low, 0.0).astype(BF16))
    request_ref[...] = (high_of * 64.0 + low_of).astype(jnp.int32) - 1


def slot_index(owner, offset, owners, capacity):
    length = owner.shape[1]
    return pl.pallas_call(
        index_kernel,
        out_shape=(
            jax.ShapeDtypeStruct((1, length), jnp.int32),
            jax.ShapeDtypeStruct((owners, capacity), jnp.int32),
        ),
        compiler_params=pltpu.CompilerParams(vmem_limit_bytes=8 << 20),
        name="slot_index",
    )(owner, offset)


def lookup_kernel(request_ref, table_ref, out_ref, asked_ref, low_ref, high_ref):
    owners, capacity = request_ref.shape
    slots = owners * capacity
    lanes = 128
    step = pl.program_id(0)
    some = table_ref.shape[0]

    @pl.when(step == 0)
    def _():
        asked_ref[...] = jnp.concatenate(
            [request_ref[at : at + 1, :] for at in range(owners)], axis=1
        )
        asked = jnp.maximum(request_ref[...] + 1, 0)
        split = jnp.concatenate([(asked >> 6).astype(F32), (asked & 63).astype(F32)], axis=1)
        weight = jnp.where(
            lax.broadcasted_iota(jnp.int32, (2 * capacity, lanes), 0) < capacity, 64.0, 1.0
        ).astype(BF16)
        block = 256

        for index in range(slots // block):
            first = index * block
            slot_of = first + lax.broadcasted_iota(jnp.int32, (block, owners), 0)
            owner_at = lax.broadcasted_iota(jnp.int32, (block, owners), 1)
            pick = (slot_of // capacity == owner_at).astype(F32)
            spread = nn_dot(pick.astype(BF16), split.astype(BF16))
            place_at = lax.rem(
                first + lax.broadcasted_iota(jnp.int32, (block, 2 * capacity), 0), capacity
            )
            lane_at = lax.rem(lax.broadcasted_iota(jnp.int32, (block, 2 * capacity), 1), capacity)
            spread = jnp.where(place_at == lane_at, spread, 0.0).astype(BF16)
            wanted = nn_dot(spread, weight).astype(jnp.int32) - 1
            lane_row = lax.broadcasted_iota(jnp.int32, (block, lanes), 1)
            rows = slice(first, first + block)
            high_ref[rows] = (wanted >> 7).astype(F32).astype(BF16)
            low_ref[rows] = ((wanted & (lanes - 1)) == lane_row).astype(F32).astype(BF16)

    first = step * (some // lanes)

    @pl.when(step == 0)
    def _():
        out_ref[...] = jnp.zeros(out_ref.shape, BF16)

    low, high = low_ref[...], high_ref[...]
    none = jnp.zeros_like(low)
    hot = [
        jnp.where(high == (first + at).astype(F32).astype(BF16), low, none)
        for at in range(some // lanes)
    ]
    chunk = table_ref[...].astype(BF16)
    out_ref[...] += nn_dot(jnp.concatenate(hot, axis=1), chunk).astype(BF16)


def look_up(requested, table):
    owners, capacity = requested.shape
    rows, width = table.shape
    slots = owners * capacity
    some = rows // 4
    return pl.pallas_call(
        lookup_kernel,
        grid=(rows // some,),
        in_specs=[
            pl.BlockSpec((owners, capacity), lambda i: (0, 0)),
            pl.BlockSpec((some, width), lambda i: (i, 0)),
        ],
        out_specs=[
            pl.BlockSpec((slots, width), lambda i: (0, 0)),
            pl.BlockSpec((1, slots), lambda i: (0, 0)),
        ],
        out_shape=[
            jax.ShapeDtypeStruct((slots, width), BF16),
            jax.ShapeDtypeStruct((1, slots), jnp.int32),
        ],
        scratch_shapes=[
            pltpu.VMEM((slots, 128), BF16),
            pltpu.VMEM((slots, 128), BF16),
        ],
        compiler_params=pltpu.CompilerParams(vmem_limit_bytes=62 << 20),
        name="look_up",
    )(requested, table)


def update_kernel(request_ref, stale_ref, incoming_ref, table_ref, out_ref, low_ref, high_ref):
    block = out_ref.shape[0]
    group, slots = low_ref.shape

    @pl.when(pl.program_id(0) == 0)
    def _():
        asked = request_ref[...]
        row = lax.broadcasted_iota(jnp.int32, (group, slots), 0)
        low_ref[...] = ((asked & (group - 1)) == row).astype(F32).astype(BF16)
        high_ref[...] = jnp.broadcast_to((asked >> (group.bit_length() - 1)).astype(F32), high_ref.shape).astype(BF16)

    low = low_ref[...]
    high = jnp.concatenate([high_ref[...]] * (group // high_ref.shape[0]), axis=0)
    none = jnp.zeros_like(low)
    first = pl.program_id(0) * (block // group)
    hot = [
        jnp.where(high == (first + at).astype(F32).astype(BF16), low, none)
        for at in range(block // group)
    ]
    table_grad = nn_dot(jnp.concatenate(hot, axis=0), incoming_ref[...])
    stale = [as_column(stale_ref[0, at : at + 1, :]) for at in range(stale_ref.shape[1])]
    rate = 0.5 / (1.0 + jnp.concatenate(stale, axis=0))
    out_ref[...] = table_ref[...] - rate * table_grad


def update_table(requested, staleness, incoming, table):
    rows, width = table.shape
    slots = incoming.shape[0]
    block, group = 1024, 256
    return pl.pallas_call(
        update_kernel,
        grid=(rows // block,),
        in_specs=[
            pl.BlockSpec((1, slots), lambda i: (0, 0)),
            pl.BlockSpec((1, block // 128, 128), lambda i: (i, 0, 0)),
            pl.BlockSpec((slots, width), lambda i: (0, 0)),
            pl.BlockSpec((block, width), lambda i: (i, 0)),
        ],
        out_specs=pl.BlockSpec((block, width), lambda i: (i, 0)),
        out_shape=jax.ShapeDtypeStruct((rows, width), F32),
        scratch_shapes=[pltpu.VMEM((group, slots), BF16), pltpu.VMEM((16, slots), BF16)],
        compiler_params=pltpu.CompilerParams(vmem_limit_bytes=62 << 20),
        name="update_table",
    )(requested, staleness.reshape(rows // block, block // 128, 128), incoming, table)


def swap(payload, axes):
    return lax.all_to_all(payload, axes, split_axis=0, concat_axis=0, tiled=True)


def axis_bits(name):
    size = lax.axis_size(name)
    return [1 << bit for bit in range(size.bit_length() - 1)]


def trade(payload, name, flip):
    size = lax.axis_size(name)
    return lax.ppermute(payload, name, [(at, at ^ flip) for at in range(size)])


def spread_plane(piece):
    whole = piece[None]
    for bit in reversed(axis_bits("emb")):
        other = trade(whole, "emb", bit)
        upper = (lax.axis_index("emb") & bit) != 0
        first = jnp.where(upper, other, whole)
        second = jnp.where(upper, whole, other)
        whole = jnp.stack([first, second], axis=1).reshape((-1,) + piece.shape)
    return whole


def gather_weights(w_proj, w_out):
    fsdp_count = lax.axis_size("fsdp")
    emb_count = lax.axis_size("emb")
    layers, rows, _ = w_proj.shape
    piece = layers * rows // emb_count
    first = lax.axis_index("emb") * piece
    mine = jnp.concatenate(
        [
            lax.dynamic_slice_in_dim(shard.reshape(layers * rows, -1), first, piece, 0)
            for shard in (w_proj, w_out)
        ],
        axis=1,
    )
    taken = [mine] + [trade(mine, "fsdp", flip) for flip in range(1, fsdp_count)]
    index = lax.axis_index("fsdp")
    across = []
    for want in range(fsdp_count):
        chosen = taken[0]
        for flip in range(1, fsdp_count):
            chosen = jnp.where((index ^ flip) == want, taken[flip], chosen)
        across.append(chosen)
    every = spread_plane(jnp.stack(across))
    per = emb_count // layers
    whole = every.reshape(layers, per, fsdp_count, piece, -1).transpose(0, 2, 1, 3, 4)
    return whole.reshape(layers, fsdp_count * rows, -1)


def turn_bits(index, count):
    bits = count.bit_length() - 1
    return sum(((index >> bit) & 1) << (bits - 1 - bit) for bit in range(bits))


def weight_pieces(gw_proj, gw_out, turned):
    if len(gw_proj.shape) == 4:
        return gw_proj
    fsdp_count = lax.axis_size("fsdp")
    emb_count = lax.axis_size("emb")
    rows = gw_proj.shape[0] // fsdp_count
    cols = gw_proj.shape[1] // emb_count
    proj = gw_proj.reshape(fsdp_count, rows, emb_count, cols).transpose(2, 0, 1, 3)
    out = gw_out.reshape(fsdp_count, emb_count, rows // emb_count, -1, cols)
    out = out.transpose(1, 0, 3, 2, 4).reshape(emb_count, fsdp_count, -1, cols)
    pieces = jnp.concatenate([proj, out], axis=2)
    pieces = jnp.take(pieces, jnp.arange(fsdp_count) ^ lax.axis_index("fsdp"), axis=1)
    if turned:
        order = turn_bits(jnp.arange(emb_count), emb_count) ^ lax.axis_index("emb")
        pieces = jnp.take(pieces, order, axis=0)
    return pieces


def plane_sum_whole(pieces):
    return swap(pieces, "emb").astype(F32).sum(axis=0)


def plane_sum_halving(pieces):
    held = pieces
    for bit in axis_bits("emb"):
        half = held.shape[0] // 2
        got = trade(held[half:].astype(BF16), "emb", bit)
        held = held[:half].astype(F32) + got.astype(F32)
    return held[0]


def finish_weights(planes, scale):
    total = planes[0]
    held = planes.astype(BF16)
    for flip in range(1, planes.shape[0]):
        total = total + trade(held[flip], "fsdp", flip).astype(F32)
    return spread_plane((total * scale).astype(BF16))


def unpack_weights(every, rows, width):
    emb_count = every.shape[0]
    proj = every[:, :rows].transpose(1, 0, 2).reshape(rows, -1)
    out = every[:, rows:].reshape(emb_count, -1, rows // emb_count, every.shape[2])
    out = out.transpose(0, 2, 1, 3).reshape(rows, width)
    return proj.astype(F32), out.astype(F32)


BLOCK = 256


def normalize(value):
    center = value - jnp.mean(value, axis=-1, keepdims=True)
    inverse = lax.rsqrt(jnp.mean(center * center, axis=-1, keepdims=True) + EPSILON)
    return center * inverse, inverse


def norm_back(gradient, normed, inverse):
    return inverse * (
        gradient
        - jnp.mean(gradient, axis=-1, keepdims=True)
        - normed * jnp.mean(gradient * normed, axis=-1, keepdims=True)
    )


def each_block(blocks, step):
    group = 2 if blocks % 2 == 0 else 1

    def some(index, carry):
        for at in range(group):
            step(index * group + at, carry)
        return carry

    lax.fori_loop(0, blocks // group, some, 0)


def rows_at(index, size=BLOCK):
    return pl.ds(pl.multiple_of(index * size, size), size)


def head_masks(width):
    lane = lax.broadcasted_iota(jnp.int32, (1, width), 1) // DH
    return [(lane == head).astype(F32).astype(BF16) for head in range(width // DH)]


def fill_stack(ref, index, value, masks):
    for head, mask in enumerate(masks):
        ref[index, head * BLOCK : (head + 1) * BLOCK, :] = value * mask


def project(hidden_ref, weight, bufs, masks, keep):
    width = hidden_ref.shape[1]
    unit = 0.5 * DH ** (-0.5)

    def step(index, carry):
        rows = rows_at(index)
        normed, _ = normalize(hidden_ref[rows].astype(F32))
        normed = 0.5 * normed
        if keep:
            bufs["normed"][:, rows] = normed.T.astype(BF16)
        half = nn_dot(normed.astype(BF16), weight[:, : 4 * width])
        grown = 1.0 + jnp.tanh(half)
        out = (half * grown).astype(BF16)
        if keep:
            grown = grown.astype(BF16)
            bufs["slope"][rows] = grown + out * (2.0 - grown)
        values = out[:, width : 2 * width]
        queries = out[:, 2 * width : 3 * width] * BF16(unit)
        keys = out[:, 3 * width :]
        bufs["gate"][rows] = out[:, :width]
        bufs["keys"][rows] = keys
        bufs["queries"][rows] = queries
        fill_stack(bufs["q_stack"], index, queries, masks)
        fill_stack(bufs["v_stack"], index, values, masks)
        if keep:
            fill_stack(bufs["k_stack"], index, keys, masks)
            bufs["keys_t"][:, rows] = (keys * BF16(unit)).T
        return carry

    each_block(hidden_ref.shape[0] // BLOCK, step)


def attend(mix_ref, bufs, heads):
    blocks = mix_ref.shape[0] // BLOCK
    ahead = lax.broadcasted_iota(jnp.int32, (BLOCK, BLOCK), 1) - lax.broadcasted_iota(
        jnp.int32, (BLOCK, BLOCK), 0
    )

    def clear(index, carry):
        mix_ref[rows_at(index)] = jnp.zeros((BLOCK, mix_ref.shape[1]), F32)
        return carry

    lax.fori_loop(0, blocks, clear, 0)

    def pair(at, to):
        keys = bufs["keys"][rows_at(to)]
        visible = (ahead <= (at - to) * BLOCK).astype(F32).astype(BF16)
        parts = []
        halves = nt_dot(bufs["q_stack"][at], keys).astype(BF16)
        for head in range(heads):
            half = halves[head * BLOCK : (head + 1) * BLOCK]
            parts.append(half * visible * (1.0 + jnp.tanh(half)))
        return nn_dot(jnp.concatenate(parts, axis=1), bufs["v_stack"][to])

    def add(at, to, total):
        mix_ref[rows_at(at)] += total

    each_pair(blocks, pair, add)


def each_pair(blocks, pair, add):
    count = blocks * (blocks + 1) // 2
    group = 5 if count % 5 == 0 else 1

    def step(index, place):
        at, to = place
        work = []
        for _ in range(group):
            work.append((at, to, pair(at, to)))
            done = to == at
            to = jnp.where(done, 0, to + 1)
            at = jnp.where(done, at + 1, at)
        for item in work:
            add(*item)
        return at, to

    lax.fori_loop(0, count // group, step, (jnp.int32(0), jnp.int32(0)))


def finish_forward(hidden_ref, mix_ref, weight, gate_ref, next_ref):
    width = hidden_ref.shape[1]

    def step(index, carry):
        rows = rows_at(index)
        mixed, _ = normalize(mix_ref[rows])
        gated = (mixed * gate_ref[rows].astype(F32)).astype(BF16)
        branch = nn_dot(gated, weight[:, 4 * width :])
        next_ref[rows] = (hidden_ref[rows].astype(F32) + branch).astype(BF16)
        return carry

    lax.fori_loop(0, hidden_ref.shape[0] // BLOCK, step, 0)


def backward(hidden_ref, grad_in, grad_out, weight, mix_ref, gw_proj_ref, gw_out_ref, bufs, masks, here, flip):
    length, width = hidden_ref.shape
    heads = len(masks)
    blocks = length // BLOCK
    slope_ref, gpre_ref, gm_ref = bufs["slope"], bufs["gpre"], bufs["gm"]

    def enter(index, carry):
        rows = rows_at(index)
        gradient = grad_in[rows].astype(BF16)
        mixed, inverse = normalize(mix_ref[rows])
        gate = bufs["gate"][rows].astype(F32)
        gated = mixed * gate
        bufs["gated"][:, rows] = gated.T.astype(BF16)
        grad_gated = nt_dot(gradient, weight[:, 4 * width :])
        gpre_ref[rows, :width] = (grad_gated * mixed).astype(BF16) * slope_ref[rows, :width]
        grad_mix = norm_back(grad_gated * gate, mixed, inverse).astype(BF16)
        gm_ref[rows] = grad_mix
        fill_stack(bufs["g_stack"], index, grad_mix, masks)
        bufs["gq"][:, rows] = jnp.zeros((width, BLOCK), F32)
        bufs["gv"][rows] = jnp.zeros((BLOCK, width), F32)
        bufs["gk"][rows] = jnp.zeros((BLOCK, width), F32)
        bufs["round"][rows] = gradient
        return carry

    each_block(blocks, enter)
    store_out_pieces(gw_out_ref, gw_proj_ref, nn_dot(bufs["gated"][...], bufs["round"][...]), here, flip)
    ahead = lax.broadcasted_iota(jnp.int32, (BLOCK, BLOCK), 0) - lax.broadcasted_iota(
        jnp.int32, (BLOCK, BLOCK), 1
    )

    def pair(at, to):
        keys_at, cols = rows_at(to), rows_at(at)
        visible = (ahead <= (at - to) * BLOCK).astype(F32).astype(BF16)
        attns, grads, turned = [], [], []
        halves = nt_dot(bufs["k_stack"][to], bufs["queries"][cols]).astype(BF16)
        grad_attns = nt_dot(bufs["v_stack"][to], gm_ref[cols]).astype(BF16)
        for head in range(heads):
            span = slice(head * BLOCK, (head + 1) * BLOCK)
            half = halves[span]
            turn = jnp.tanh(half)
            grown = 1.0 + turn
            attn = half * grown
            attns.append(attn * visible)
            grads.append(grad_attns[span] * visible * (grown + attn * (1.0 - turn)))
            place = slice(head * DH, (head + 1) * DH)
            turned.append(nn_dot(bufs["keys_t"][place, keys_at], grads[-1]))
        return (
            nn_dot(jnp.concatenate(attns, axis=1), bufs["g_stack"][at]),
            nn_dot(jnp.concatenate(grads, axis=1), bufs["q_stack"][at]),
            turned,
        )

    def add(at, to, totals):
        keys_at, cols = rows_at(to), rows_at(at)
        bufs["gv"][keys_at] += totals[0]
        bufs["gk"][keys_at] += totals[1]
        for head in range(heads):
            bufs["gq"][head * DH : (head + 1) * DH, cols] += totals[2][head]

    each_pair(blocks, pair, add)

    def leave(index, carry):
        rows = rows_at(index)
        for at, grad in enumerate((bufs["gv"][rows], bufs["gq"][:, rows].T, bufs["gk"][rows])):
            cols = slice((at + 1) * width, (at + 2) * width)
            gpre_ref[rows, cols] = grad.astype(BF16) * slope_ref[rows, cols]
        grad_normed = nt_dot(gpre_ref[rows, :], weight[:, : 4 * width])
        normed, inverse = normalize(hidden_ref[rows].astype(F32))
        gradient = grad_in[rows].astype(F32) + norm_back(grad_normed, normed, 0.5 * inverse)
        grad_out[rows] = gradient.astype(grad_out.dtype)
        return carry

    each_block(blocks, leave)

    def weigh(index, carry):
        cols = rows_at(index)
        grad = nn_dot(bufs["normed"][...], gpre_ref[:, cols]).astype(BF16)
        if len(gw_proj_ref.shape) == 2:
            gw_proj_ref[:, cols] = grad
            return carry
        peers, shards, _, lanes = gw_proj_ref.shape
        deep = width // shards
        for part in range(BLOCK // lanes):
            for shard in range(shards):
                slot = peer_slot(index * (BLOCK // lanes) + part, peers, here, flip)
                gw_proj_ref[slot, shard ^ here[0], :deep, :] = grad[
                    shard * deep : (shard + 1) * deep, part * lanes : (part + 1) * lanes
                ]
        return carry

    lax.fori_loop(0, 4 * width // BLOCK, weigh, 0)


def peer_slot(peer, peers, here, flip):
    return turn_bits(peer ^ here[1], peers) if flip else peer


def store_out_pieces(gw_out_ref, gw_proj_ref, grad, here, flip):
    if len(gw_proj_ref.shape) == 2:
        gw_out_ref[...] = grad.astype(BF16)
        return
    peers, shards, rows, lanes = gw_proj_ref.shape
    width = grad.shape[0]
    deep = width // shards
    some = deep // peers
    for shard in range(shards):
        for peer in range(peers):
            first = shard * deep + peer * some
            piece = [
                grad[first : first + some, at : at + lanes] for at in range(0, width, lanes)
            ]
            gw_proj_ref[peer_slot(peer, peers, here, flip), shard ^ here[0], deep:rows, :] = jnp.concatenate(piece, axis=0).astype(BF16)
    gw_out_ref[...] = jnp.zeros(gw_out_ref.shape, BF16)


def weight_shapes(width, shards, peers):
    deep = width // shards
    lanes = 4 * width // peers
    if lanes == 128 and deep // peers == 8 and deep % 16 == 0:
        rows = deep + deep // peers * width // lanes
        return [
            jax.ShapeDtypeStruct((peers, shards, rows, lanes), BF16),
            jax.ShapeDtypeStruct((8, 128), BF16),
        ]
    return [
        jax.ShapeDtypeStruct((width, 4 * width), BF16),
        jax.ShapeDtypeStruct((width, width), BF16),
    ]


def layer_buffers(length, width):
    heads = width // DH
    blocks = length // BLOCK
    stack = pltpu.VMEM((blocks, heads * BLOCK, width), BF16)
    plain = pltpu.VMEM((length, width), BF16)
    turned = pltpu.VMEM((width, length), BF16)
    return dict(
        slope=pltpu.VMEM((length, 4 * width), BF16),
        gpre=pltpu.VMEM((length, 4 * width), BF16),
        normed=turned,
        gated=turned,
        keys_t=turned,
        gq=pltpu.VMEM((width, length), F32),
        gv=pltpu.VMEM((length, width), F32),
        gk=pltpu.VMEM((length, width), F32),
        gate=plain,
        keys=plain,
        queries=plain,
        gm=plain,
        round=plain,
        q_stack=stack,
        k_stack=stack,
        v_stack=stack,
        g_stack=stack,
    )


def top_kernel(names, layers, here_ref, target_ref, rows_ref, weights_ref, cot_ref, *refs):
    hidden_refs, refs = refs[:layers], refs[layers:]
    mix_refs, refs = refs[: layers - 1], refs[layers - 1 :]
    grad_ref, gw_proj_ref, gw_out_ref, last_mix_ref, low_ref, high_ref = refs[:6]
    bufs = dict(zip(names, refs[6:]))
    width = rows_ref.shape[1]
    masks = head_masks(width)
    place(target_ref, rows_ref, hidden_refs[0], low_ref, high_ref)
    for layer in range(layers):
        last = layer == layers - 1
        weight = weights_ref.at[layer]
        mix_ref = last_mix_ref if last else mix_refs[layer]
        project(hidden_refs[layer], weight, bufs, masks, last)
        attend(mix_ref, bufs, len(masks))
        if not last:
            finish_forward(
                hidden_refs[layer], mix_ref, weight, bufs["gate"], hidden_refs[layer + 1]
            )
    backward(
        hidden_refs[-1],
        cot_ref,
        grad_ref,
        weights_ref.at[layers - 1],
        last_mix_ref,
        gw_proj_ref,
        gw_out_ref,
        bufs,
        masks,
        (here_ref[0], here_ref[1]),
        False,
    )


def place(target_ref, rows_ref, out_ref, low_ref, high_ref):
    length = out_ref.shape[0]
    lanes = 128
    for at in range(0, length, lanes):
        rows = slice(at, at + lanes)
        wanted = as_column(target_ref[:, rows]).astype(jnp.int32)
        wanted = jnp.broadcast_to(wanted, (lanes, lanes))
        high_ref[rows] = (wanted >> 7).astype(F32).astype(BF16)
        lane_row = lax.broadcasted_iota(jnp.int32, (lanes, lanes), 1)
        low_ref[rows] = ((wanted & (lanes - 1)) == lane_row).astype(F32).astype(BF16)
    out_ref[...] = jnp.zeros(out_ref.shape, BF16)

    def step(index, carry):
        low, high = low_ref[...], high_ref[...]
        none = jnp.zeros_like(low)
        hot = [
            jnp.where(high == (2 * index + side).astype(F32).astype(BF16), low, none)
            for side in range(2)
        ]
        chunk = rows_ref[rows_at(index, 2 * lanes)]
        out_ref[...] += nn_dot(jnp.concatenate(hot, axis=1), chunk).astype(BF16)
        return carry

    lax.fori_loop(0, rows_ref.shape[0] // (2 * lanes), step, 0)


def in_memory(count):
    whole = pl.BlockSpec(memory_space=pltpu.VMEM)
    return [pl.BlockSpec(memory_space=pltpu.SMEM)] + [whole] * (count - 1)


def run_top(here, target, rows, weights, cotangent, shards, peers):
    layers = weights.shape[0]
    length, width = cotangent.shape
    buffers = layer_buffers(length, width)
    hidden = jax.ShapeDtypeStruct((length, width), BF16)
    wide = jax.ShapeDtypeStruct((length, width), F32)
    return pl.pallas_call(
        functools.partial(top_kernel, tuple(buffers), layers),
        in_specs=in_memory(5),
        out_shape=[hidden] * layers
        + [wide] * (layers - 1)
        + [wide]
        + weight_shapes(width, shards, peers),
        scratch_shapes=[pltpu.VMEM((length, width), F32)]
        + [pltpu.VMEM((length, 128), BF16)] * 2
        + list(buffers.values()),
        compiler_params=pltpu.CompilerParams(vmem_limit_bytes=62 << 20),
        name="forward_and_last_backward",
    )(here, target, rows, weights, cotangent)


def lower_kernel(
    names, layer, here_ref, target_ref, hidden_ref, mix_ref, weights_ref, grad_ref, out_ref, gw_proj_ref, gw_out_ref, done_ref, *refs
):
    bufs = dict(zip(names, refs))
    masks = head_masks(hidden_ref.shape[1])
    weight = weights_ref.at[layer]
    project(hidden_ref, weight, bufs, masks, True)
    first = layer == 0
    backward(
        hidden_ref,
        grad_ref,
        done_ref if first else out_ref,
        weight,
        mix_ref,
        gw_proj_ref,
        gw_out_ref,
        bufs,
        masks,
        (here_ref[0], here_ref[1]),
        True,
    )
    if not first:
        return
    length = hidden_ref.shape[0]

    target = jnp.broadcast_to(target_ref[...], (BLOCK, length))
    slot_row = lax.broadcasted_iota(jnp.int32, (BLOCK, length), 0)
    low = ((target & (BLOCK - 1)) == slot_row).astype(F32).astype(BF16)
    high = (target >> (BLOCK.bit_length() - 1)).astype(F32).astype(BF16)
    none = jnp.zeros_like(low)
    group = 4 * BLOCK

    def send(index, carry):
        hot = [
            jnp.where(high == (4 * index + at).astype(F32).astype(BF16), low, none)
            for at in range(4)
        ]
        out_ref[rows_at(index, group)] = nn_dot(
            jnp.concatenate(hot, axis=0), done_ref[...]
        ).astype(BF16)
        return carry

    lax.fori_loop(0, out_ref.shape[0] // group, send, 0)


def run_lower(layer, here, target, hidden, mix, weights, gradient, slots, shards, peers):
    length, width = hidden.shape
    buffers = layer_buffers(length, width)
    result = (
        jax.ShapeDtypeStruct((slots, width), BF16)
        if layer == 0
        else jax.ShapeDtypeStruct((length, width), F32)
    )
    return pl.pallas_call(
        functools.partial(lower_kernel, tuple(buffers), layer),
        in_specs=in_memory(6),
        out_shape=[result] + weight_shapes(width, shards, peers),
        scratch_shapes=[pltpu.VMEM((length, width), BF16)] + list(buffers.values()),
        compiler_params=pltpu.CompilerParams(vmem_limit_bytes=62 << 20),
        name="lower_backward",
    )(here, target, hidden, mix, weights, gradient)


def local(item_table, item_owner, item_row, staleness, w_proj, w_out, out_grad):
    fsdp_count = lax.axis_size("fsdp")
    emb_count = lax.axis_size("emb")
    owners = fsdp_count * emb_count
    length = item_row.shape[1]
    capacity = 2 * length // owners
    width = item_table.shape[1]
    layer_count, shard_rows, _ = w_proj.shape
    slots = owners * capacity
    both = ("fsdp", "emb")
    weights = gather_weights(w_proj, w_out)
    target, request = slot_index(item_owner.reshape(1, length), item_row, owners, capacity)
    requested = swap(request, both)
    looked_up, asked = look_up(requested.reshape(owners, capacity), item_table)
    returned = swap(looked_up.reshape(owners, capacity, width), both)
    returned = returned.reshape(slots, width)
    here = jnp.stack([lax.axis_index("fsdp"), lax.axis_index("emb")]).astype(jnp.int32)
    norm_scale = (owners * length) ** (-0.5)
    outs = run_top(here, target, returned, weights, out_grad[0], fsdp_count, emb_count)
    hiddens, mixes = outs[:layer_count], outs[layer_count : 2 * layer_count - 1]
    gradient, gw_proj, gw_out = outs[2 * layer_count - 1 :]
    planes = [plane_sum_whole(weight_pieces(gw_proj, gw_out, False))]
    for layer in reversed(range(layer_count - 1)):
        gradient, gw_proj, gw_out = run_lower(
            layer,
            here,
            target,
            hiddens[layer],
            mixes[layer],
            weights,
            gradient,
            slots,
            fsdp_count,
            emb_count,
        )
        pieces = weight_pieces(gw_proj, gw_out, True)
        planes.insert(0, plane_sum_halving(pieces))
    incoming = swap(gradient.reshape(owners, capacity, width), both)
    incoming = incoming.reshape(slots, width)
    new_table = update_table(asked, staleness, incoming, item_table)
    every = finish_weights(jnp.stack(planes, axis=1), norm_scale)
    sums = [unpack_weights(every[:, at], shard_rows, width) for at in range(layer_count)]
    return (
        new_table,
        jnp.stack([proj for proj, _ in sums]),
        jnp.stack([out for _, out in sums]),
    )


def solution(mesh):
    return jax.shard_map(
        local,
        mesh=mesh,
        in_specs=(
            P(("fsdp", "emb"), None),
            P(("fsdp", "emb"), None, None),
            P(("fsdp", "emb"), None),
            P(("fsdp", "emb")),
            P(None, "fsdp", None),
            P(None, "fsdp", None),
            P(("fsdp", "emb"), None, None),
        ),
        out_specs=(P(("fsdp", "emb"), None), P(None, "fsdp", None), P(None, "fsdp", None)),
        check_vma=False,
    )
```

```python
import functools

import jax
import jax.numpy as jnp
from jax import lax
from jax.experimental import pallas as pl
from jax.experimental.pallas import tpu as pltpu
from jax.sharding import PartitionSpec as P

DH = 64
EPSILON = 1e-05
F32 = jnp.float32
BF16 = jnp.bfloat16


def nt_dot(a, b):
    return lax.dot_general(a, b, (((1,), (1,)), ((), ())), preferred_element_type=F32)


def nn_dot(a, b):
    return jnp.dot(a, b, preferred_element_type=F32)


def as_column(row):
    side = row.shape[1]
    same = lax.broadcasted_iota(jnp.int32, (side, side), 0) == lax.broadcasted_iota(
        jnp.int32, (side, side), 1
    )
    return jnp.sum(jnp.where(same, row.astype(F32), 0.0), axis=1, keepdims=True)


def index_kernel(owner_ref, row_ref, target_ref, request_ref):
    owners, capacity = request_ref.shape
    length = owner_ref.shape[1]
    lane = 128
    owner = owner_ref[...]
    member = (lax.broadcasted_iota(jnp.int32, (owners, length), 0) == owner).astype(F32)
    blocks = [member[:, at : at + lane] for at in range(0, length, lane)]
    stacked = jnp.concatenate(blocks, axis=0).astype(BF16)
    upper = (
        lax.broadcasted_iota(jnp.int32, (lane, lane), 0)
        < lax.broadcasted_iota(jnp.int32, (lane, lane), 1)
    ).astype(F32).astype(BF16)
    inside = nn_dot(stacked, upper)
    base = jnp.zeros((owners, 1), F32)
    slots = []
    for at, block in enumerate(blocks):
        earlier = inside[at * owners : (at + 1) * owners] + base
        slots.append(jnp.sum(earlier * block, axis=0, keepdims=True))
        base = base + jnp.sum(block, axis=1, keepdims=True)
    slot = jnp.concatenate(slots, axis=1).astype(jnp.int32)
    target_ref[...] = owner * capacity + slot
    value = row_ref[...] + 1
    high = (value >> 6).astype(F32)
    low = (value & 63).astype(F32)
    here = lax.broadcasted_iota(jnp.int32, (capacity, length), 0) == slot
    members = member.astype(BF16)
    high_of = nt_dot(members, jnp.where(here, high, 0.0).astype(BF16))
    low_of = nt_dot(members, jnp.where(here, low, 0.0).astype(BF16))
    request_ref[...] = (high_of * 64.0 + low_of).astype(jnp.int32) - 1


def slot_index(owner, offset, owners, capacity):
    length = owner.shape[1]
    return pl.pallas_call(
        index_kernel,
        out_shape=(
            jax.ShapeDtypeStruct((1, length), jnp.int32),
            jax.ShapeDtypeStruct((owners, capacity), jnp.int32),
        ),
        compiler_params=pltpu.CompilerParams(vmem_limit_bytes=62 << 20),
        name="slot_index",
    )(owner, offset)


def lookup_kernel(request_ref, table_ref, out_ref, asked_ref, low_ref, high_ref):
    owners, capacity = request_ref.shape
    slots = owners * capacity
    lanes = 128
    step = pl.program_id(0)
    some = table_ref.shape[0]

    @pl.when(step == 0)
    def _():
        asked_ref[...] = jnp.concatenate(
            [request_ref[at : at + 1, :] for at in range(owners)], axis=1
        )
        asked = jnp.maximum(request_ref[...] + 1, 0)
        split = jnp.concatenate([(asked >> 6).astype(F32), (asked & 63).astype(F32)], axis=1)
        weight = jnp.where(
            lax.broadcasted_iota(jnp.int32, (2 * capacity, lanes), 0) < capacity, 64.0, 1.0
        ).astype(BF16)
        block = 256

        for index in range(slots // block):
            first = index * block
            slot_of = first + lax.broadcasted_iota(jnp.int32, (block, owners), 0)
            owner_at = lax.broadcasted_iota(jnp.int32, (block, owners), 1)
            pick = (slot_of // capacity == owner_at).astype(F32)
            spread = nn_dot(pick.astype(BF16), split.astype(BF16))
            place_at = lax.rem(
                first + lax.broadcasted_iota(jnp.int32, (block, 2 * capacity), 0), capacity
            )
            lane_at = lax.rem(lax.broadcasted_iota(jnp.int32, (block, 2 * capacity), 1), capacity)
            spread = jnp.where(place_at == lane_at, spread, 0.0).astype(BF16)
            wanted = nn_dot(spread, weight).astype(jnp.int32) - 1
            lane_row = lax.broadcasted_iota(jnp.int32, (block, lanes), 1)
            rows = slice(first, first + block)
            high_ref[rows] = (wanted >> 7).astype(F32).astype(BF16)
            low_ref[rows] = ((wanted & (lanes - 1)) == lane_row).astype(F32).astype(BF16)

    first = step * (some // lanes)

    @pl.when(step == 0)
    def _():
        out_ref[...] = jnp.zeros(out_ref.shape, BF16)

    low, high = low_ref[...], high_ref[...]
    none = jnp.zeros_like(low)
    hot = [
        jnp.where(high == (first + at).astype(F32).astype(BF16), low, none)
        for at in range(some // lanes)
    ]
    chunk = table_ref[...].astype(BF16)
    out_ref[...] += nn_dot(jnp.concatenate(hot, axis=1), chunk).astype(BF16)


def look_up(requested, table):
    owners, capacity = requested.shape
    rows, width = table.shape
    slots = owners * capacity
    some = rows // 4
    return pl.pallas_call(
        lookup_kernel,
        grid=(rows // some,),
        in_specs=[
            pl.BlockSpec((owners, capacity), lambda i: (0, 0)),
            pl.BlockSpec((some, width), lambda i: (i, 0)),
        ],
        out_specs=[
            pl.BlockSpec((slots, width), lambda i: (0, 0)),
            pl.BlockSpec((1, slots), lambda i: (0, 0)),
        ],
        out_shape=[
            jax.ShapeDtypeStruct((slots, width), BF16),
            jax.ShapeDtypeStruct((1, slots), jnp.int32),
        ],
        scratch_shapes=[
            pltpu.VMEM((slots, 128), BF16),
            pltpu.VMEM((slots, 128), BF16),
        ],
        compiler_params=pltpu.CompilerParams(vmem_limit_bytes=62 << 20),
        name="look_up",
    )(requested, table)


def update_kernel(request_ref, stale_ref, incoming_ref, table_ref, out_ref, low_ref, high_ref):
    block = out_ref.shape[0]
    group, slots = low_ref.shape

    @pl.when(pl.program_id(0) == 0)
    def _():
        asked = request_ref[...]
        row = lax.broadcasted_iota(jnp.int32, (group, slots), 0)
        low_ref[...] = ((asked & (group - 1)) == row).astype(F32).astype(BF16)
        high_ref[...] = jnp.broadcast_to((asked >> (group.bit_length() - 1)).astype(F32), high_ref.shape).astype(BF16)

    low = low_ref[...]
    high = jnp.concatenate([high_ref[...]] * (group // high_ref.shape[0]), axis=0)
    none = jnp.zeros_like(low)
    first = pl.program_id(0) * (block // group)
    hot = [
        jnp.where(high == (first + at).astype(F32).astype(BF16), low, none)
        for at in range(block // group)
    ]
    table_grad = nn_dot(jnp.concatenate(hot, axis=0), incoming_ref[...])
    stale = [as_column(stale_ref[0, at : at + 1, :]) for at in range(stale_ref.shape[1])]
    rate = 0.5 / (1.0 + jnp.concatenate(stale, axis=0))
    out_ref[...] = table_ref[...] - rate * table_grad


def update_table(requested, staleness, incoming, table):
    rows, width = table.shape
    slots = incoming.shape[0]
    block, group = 1024, 256
    return pl.pallas_call(
        update_kernel,
        grid=(rows // block,),
        in_specs=[
            pl.BlockSpec((1, slots), lambda i: (0, 0)),
            pl.BlockSpec((1, block // 128, 128), lambda i: (i, 0, 0)),
            pl.BlockSpec((slots, width), lambda i: (0, 0)),
            pl.BlockSpec((block, width), lambda i: (i, 0)),
        ],
        out_specs=pl.BlockSpec((block, width), lambda i: (i, 0)),
        out_shape=jax.ShapeDtypeStruct((rows, width), F32),
        scratch_shapes=[pltpu.VMEM((group, slots), BF16), pltpu.VMEM((16, slots), BF16)],
        compiler_params=pltpu.CompilerParams(vmem_limit_bytes=60 << 20),
        name="update_table",
    )(requested, staleness.reshape(rows // block, block // 128, 128), incoming, table)


def swap(payload, axes):
    return lax.all_to_all(payload, axes, split_axis=0, concat_axis=0, tiled=True)


def axis_bits(name):
    size = lax.axis_size(name)
    return [1 << bit for bit in range(size.bit_length() - 1)]


def trade(payload, name, flip):
    size = lax.axis_size(name)
    return lax.ppermute(payload, name, [(at, at ^ flip) for at in range(size)])


def spread_plane(piece):
    whole = piece[None]
    for bit in reversed(axis_bits("emb")):
        other = trade(whole, "emb", bit)
        upper = (lax.axis_index("emb") & bit) != 0
        first = jnp.where(upper, other, whole)
        second = jnp.where(upper, whole, other)
        whole = jnp.stack([first, second], axis=1).reshape((-1,) + piece.shape)
    return whole


def gather_weights(w_proj, w_out):
    fsdp_count = lax.axis_size("fsdp")
    emb_count = lax.axis_size("emb")
    layers, rows, _ = w_proj.shape
    piece = layers * rows // emb_count
    first = lax.axis_index("emb") * piece
    mine = jnp.concatenate(
        [
            lax.dynamic_slice_in_dim(shard.reshape(layers * rows, -1), first, piece, 0)
            for shard in (w_proj, w_out)
        ],
        axis=1,
    )
    taken = [mine] + [trade(mine, "fsdp", flip) for flip in range(1, fsdp_count)]
    index = lax.axis_index("fsdp")
    across = []
    for want in range(fsdp_count):
        chosen = taken[0]
        for flip in range(1, fsdp_count):
            chosen = jnp.where((index ^ flip) == want, taken[flip], chosen)
        across.append(chosen)
    every = spread_plane(jnp.stack(across))
    per = emb_count // layers
    whole = every.reshape(layers, per, fsdp_count, piece, -1).transpose(0, 2, 1, 3, 4)
    return whole.reshape(layers, fsdp_count * rows, -1)


def turn_bits(index, count):
    bits = count.bit_length() - 1
    return sum(((index >> bit) & 1) << (bits - 1 - bit) for bit in range(bits))


def weight_pieces(gw_proj, gw_out, turned):
    if len(gw_proj.shape) == 4:
        return gw_proj
    fsdp_count = lax.axis_size("fsdp")
    emb_count = lax.axis_size("emb")
    rows = gw_proj.shape[0] // fsdp_count
    cols = gw_proj.shape[1] // emb_count
    proj = gw_proj.reshape(fsdp_count, rows, emb_count, cols).transpose(2, 0, 1, 3)
    out = gw_out.reshape(fsdp_count, emb_count, rows // emb_count, -1, cols)
    out = out.transpose(1, 0, 3, 2, 4).reshape(emb_count, fsdp_count, -1, cols)
    pieces = jnp.concatenate([proj, out], axis=2)
    pieces = jnp.take(pieces, jnp.arange(fsdp_count) ^ lax.axis_index("fsdp"), axis=1)
    if turned:
        order = turn_bits(jnp.arange(emb_count), emb_count) ^ lax.axis_index("emb")
        pieces = jnp.take(pieces, order, axis=0)
    return pieces


def plane_sum_whole(pieces):
    return swap(pieces, "emb").astype(F32).sum(axis=0)


def plane_sum_halving(pieces):
    held = pieces
    for bit in axis_bits("emb"):
        half = held.shape[0] // 2
        got = trade(held[half:].astype(BF16), "emb", bit)
        held = held[:half].astype(F32) + got.astype(F32)
    return held[0]


def finish_weights(planes, scale):
    total = planes[0]
    held = planes.astype(BF16)
    for flip in range(1, planes.shape[0]):
        got = trade(held[flip], "fsdp", flip)
        total = total + got.astype(F32)
    return spread_plane((total * scale).astype(BF16))


def unpack_weights(every, rows, width):
    emb_count = every.shape[0]
    proj = every[:, :rows].transpose(1, 0, 2).reshape(rows, -1)
    out = every[:, rows:].reshape(emb_count, -1, rows // emb_count, every.shape[2])
    out = out.transpose(0, 2, 1, 3).reshape(rows, width)
    return proj.astype(F32), out.astype(F32)


BLOCK = 256


def normalize(value):
    center = value - jnp.mean(value, axis=-1, keepdims=True)
    inverse = lax.rsqrt(jnp.mean(center * center, axis=-1, keepdims=True) + EPSILON)
    return center * inverse, inverse


def norm_back(gradient, normed, inverse):
    return inverse * (
        gradient
        - jnp.mean(gradient, axis=-1, keepdims=True)
        - normed * jnp.mean(gradient * normed, axis=-1, keepdims=True)
    )


def each_block(blocks, step):
    group = 2 if blocks % 2 == 0 else 1

    def some(index, carry):
        for at in range(group):
            step(index * group + at, carry)
        return carry

    lax.fori_loop(0, blocks // group, some, 0)


def rows_at(index, size=BLOCK):
    return pl.ds(pl.multiple_of(index * size, size), size)


def head_masks(width):
    lane = lax.broadcasted_iota(jnp.int32, (1, width), 1) // DH
    return [(lane == head).astype(F32).astype(BF16) for head in range(width // DH)]


def fill_stack(ref, index, value, masks):
    for head, mask in enumerate(masks):
        ref[index, head * BLOCK : (head + 1) * BLOCK, :] = value * mask


def project(hidden_ref, weight, bufs, masks, keep):
    width = hidden_ref.shape[1]
    unit = 0.5 * DH ** (-0.5)

    def step(index, carry):
        rows = rows_at(index)
        normed, _ = normalize(hidden_ref[rows].astype(F32))
        normed = 0.5 * normed
        if keep:
            bufs["normed"][:, rows] = normed.T.astype(BF16)
        half = nn_dot(normed.astype(BF16), weight[:, : 4 * width])
        grown = 1.0 + jnp.tanh(half)
        out = (half * grown).astype(BF16)
        if keep:
            grown = grown.astype(BF16)
            bufs["slope"][rows] = grown + out * (2.0 - grown)
        values = out[:, width : 2 * width]
        queries = out[:, 2 * width : 3 * width] * BF16(unit)
        keys = out[:, 3 * width :]
        bufs["gate"][rows] = out[:, :width]
        bufs["keys"][rows] = keys
        bufs["queries"][rows] = queries
        fill_stack(bufs["q_stack"], index, queries, masks)
        fill_stack(bufs["v_stack"], index, values, masks)
        if keep:
            fill_stack(bufs["k_stack"], index, keys, masks)
            bufs["keys_t"][:, rows] = (keys * BF16(unit)).T
        return carry

    each_block(hidden_ref.shape[0] // BLOCK, step)


def attend(mix_ref, bufs, heads):
    blocks = mix_ref.shape[0] // BLOCK
    ahead = lax.broadcasted_iota(jnp.int32, (BLOCK, BLOCK), 1) - lax.broadcasted_iota(
        jnp.int32, (BLOCK, BLOCK), 0
    )

    def clear(index, carry):
        mix_ref[rows_at(index)] = jnp.zeros((BLOCK, mix_ref.shape[1]), F32)
        return carry

    lax.fori_loop(0, blocks, clear, 0)

    def pair(at, to):
        keys = bufs["keys"][rows_at(to)]
        visible = (ahead <= (at - to) * BLOCK).astype(F32).astype(BF16)
        parts = []
        halves = nt_dot(bufs["q_stack"][at], keys).astype(BF16)
        for head in range(heads):
            half = halves[head * BLOCK : (head + 1) * BLOCK]
            parts.append(half * visible * (1.0 + jnp.tanh(half)))
        return nn_dot(jnp.concatenate(parts, axis=1), bufs["v_stack"][to])

    def add(at, to, total):
        mix_ref[rows_at(at)] += total

    each_pair(blocks, pair, add)


def each_pair(blocks, pair, add):
    count = blocks * (blocks + 1) // 2
    group = 5 if count % 5 == 0 else 1

    def step(index, place):
        at, to = place
        work = []
        for _ in range(group):
            work.append((at, to, pair(at, to)))
            done = to == at
            to = jnp.where(done, 0, to + 1)
            at = jnp.where(done, at + 1, at)
        for item in work:
            add(*item)
        return at, to

    lax.fori_loop(0, count // group, step, (jnp.int32(0), jnp.int32(0)))


def finish_forward(hidden_ref, mix_ref, weight, gate_ref, next_ref):
    width = hidden_ref.shape[1]

    def step(index, carry):
        rows = rows_at(index)
        mixed, _ = normalize(mix_ref[rows])
        gated = (mixed * gate_ref[rows].astype(F32)).astype(BF16)
        branch = nn_dot(gated, weight[:, 4 * width :])
        next_ref[rows] = (hidden_ref[rows].astype(F32) + branch).astype(BF16)
        return carry

    lax.fori_loop(0, hidden_ref.shape[0] // BLOCK, step, 0)


def backward(hidden_ref, grad_in, grad_out, weight, mix_ref, gw_proj_ref, gw_out_ref, bufs, masks, here, flip):
    length, width = hidden_ref.shape
    heads = len(masks)
    blocks = length // BLOCK
    slope_ref, gpre_ref, gm_ref = bufs["slope"], bufs["gpre"], bufs["gm"]

    def enter(index, carry):
        rows = rows_at(index)
        gradient = grad_in[rows].astype(BF16)
        mixed, inverse = normalize(mix_ref[rows])
        gate = bufs["gate"][rows].astype(F32)
        gated = mixed * gate
        bufs["gated"][:, rows] = gated.T.astype(BF16)
        grad_gated = nt_dot(gradient, weight[:, 4 * width :])
        gpre_ref[rows, :width] = (grad_gated * mixed).astype(BF16) * slope_ref[rows, :width]
        grad_mix = norm_back(grad_gated * gate, mixed, inverse).astype(BF16)
        gm_ref[rows] = grad_mix
        fill_stack(bufs["g_stack"], index, grad_mix, masks)
        bufs["gq"][:, rows] = jnp.zeros((width, BLOCK), F32)
        bufs["gv"][rows] = jnp.zeros((BLOCK, width), F32)
        bufs["gk"][rows] = jnp.zeros((BLOCK, width), F32)
        bufs["round"][rows] = gradient
        return carry

    each_block(blocks, enter)
    store_out_pieces(gw_out_ref, gw_proj_ref, nn_dot(bufs["gated"][...], bufs["round"][...]), here, flip)
    ahead = lax.broadcasted_iota(jnp.int32, (BLOCK, BLOCK), 0) - lax.broadcasted_iota(
        jnp.int32, (BLOCK, BLOCK), 1
    )

    def pair(at, to):
        keys_at, cols = rows_at(to), rows_at(at)
        visible = (ahead <= (at - to) * BLOCK).astype(F32).astype(BF16)
        attns, grads, turned = [], [], []
        halves = nt_dot(bufs["k_stack"][to], bufs["queries"][cols]).astype(BF16)
        grad_attns = nt_dot(bufs["v_stack"][to], gm_ref[cols]).astype(BF16)
        for head in range(heads):
            span = slice(head * BLOCK, (head + 1) * BLOCK)
            half = halves[span]
            turn = jnp.tanh(half)
            grown = 1.0 + turn
            attn = half * grown
            attns.append(attn * visible)
            grads.append(grad_attns[span] * visible * (grown + attn * (1.0 - turn)))
            place = slice(head * DH, (head + 1) * DH)
            turned.append(nn_dot(bufs["keys_t"][place, keys_at], grads[-1]))
        return (
            nn_dot(jnp.concatenate(attns, axis=1), bufs["g_stack"][at]),
            nn_dot(jnp.concatenate(grads, axis=1), bufs["q_stack"][at]),
            turned,
        )

    def add(at, to, totals):
        keys_at, cols = rows_at(to), rows_at(at)
        bufs["gv"][keys_at] += totals[0]
        bufs["gk"][keys_at] += totals[1]
        for head in range(heads):
            bufs["gq"][head * DH : (head + 1) * DH, cols] += totals[2][head]

    each_pair(blocks, pair, add)

    def leave(index, carry):
        rows = rows_at(index)
        for at, grad in enumerate((bufs["gv"][rows], bufs["gq"][:, rows].T, bufs["gk"][rows])):
            cols = slice((at + 1) * width, (at + 2) * width)
            gpre_ref[rows, cols] = grad.astype(BF16) * slope_ref[rows, cols]
        grad_normed = nt_dot(gpre_ref[rows, :], weight[:, : 4 * width])
        normed, inverse = normalize(hidden_ref[rows].astype(F32))
        gradient = grad_in[rows].astype(F32) + norm_back(grad_normed, normed, 0.5 * inverse)
        grad_out[rows] = gradient.astype(grad_out.dtype)
        return carry

    each_block(blocks, leave)

    def weigh(index, carry):
        cols = rows_at(index)
        grad = nn_dot(bufs["normed"][...], gpre_ref[:, cols]).astype(BF16)
        if len(gw_proj_ref.shape) == 2:
            gw_proj_ref[:, cols] = grad
            return carry
        peers, shards, _, lanes = gw_proj_ref.shape
        deep = width // shards
        for part in range(BLOCK // lanes):
            for shard in range(shards):
                slot = peer_slot(index * (BLOCK // lanes) + part, peers, here, flip)
                gw_proj_ref[slot, shard ^ here[0], :deep, :] = grad[
                    shard * deep : (shard + 1) * deep, part * lanes : (part + 1) * lanes
                ]
        return carry

    lax.fori_loop(0, 4 * width // BLOCK, weigh, 0)


def peer_slot(peer, peers, here, flip):
    return turn_bits(peer ^ here[1], peers) if flip else peer


def store_out_pieces(gw_out_ref, gw_proj_ref, grad, here, flip):
    if len(gw_proj_ref.shape) == 2:
        gw_out_ref[...] = grad.astype(BF16)
        return
    peers, shards, rows, lanes = gw_proj_ref.shape
    width = grad.shape[0]
    deep = width // shards
    some = deep // peers
    for shard in range(shards):
        for peer in range(peers):
            first = shard * deep + peer * some
            piece = [
                grad[first : first + some, at : at + lanes] for at in range(0, width, lanes)
            ]
            gw_proj_ref[peer_slot(peer, peers, here, flip), shard ^ here[0], deep:rows, :] = jnp.concatenate(piece, axis=0).astype(BF16)
    gw_out_ref[...] = jnp.zeros(gw_out_ref.shape, BF16)


def weight_shapes(width, shards, peers):
    deep = width // shards
    lanes = 4 * width // peers
    if lanes == 128 and deep // peers == 8 and deep % 16 == 0:
        rows = deep + deep // peers * width // lanes
        return [
            jax.ShapeDtypeStruct((peers, shards, rows, lanes), BF16),
            jax.ShapeDtypeStruct((8, 128), BF16),
        ]
    return [
        jax.ShapeDtypeStruct((width, 4 * width), BF16),
        jax.ShapeDtypeStruct((width, width), BF16),
    ]


def layer_buffers(length, width):
    heads = width // DH
    blocks = length // BLOCK
    stack = pltpu.VMEM((blocks, heads * BLOCK, width), BF16)
    plain = pltpu.VMEM((length, width), BF16)
    turned = pltpu.VMEM((width, length), BF16)
    return dict(
        slope=pltpu.VMEM((length, 4 * width), BF16),
        gpre=pltpu.VMEM((length, 4 * width), BF16),
        normed=turned,
        gated=turned,
        keys_t=turned,
        gq=pltpu.VMEM((width, length), F32),
        gv=pltpu.VMEM((length, width), F32),
        gk=pltpu.VMEM((length, width), F32),
        gate=plain,
        keys=plain,
        queries=plain,
        gm=plain,
        round=plain,
        q_stack=stack,
        k_stack=stack,
        v_stack=stack,
        g_stack=stack,
    )


def top_kernel(names, layers, here_ref, target_ref, rows_ref, weights_ref, cot_ref, *refs):
    hidden_refs, refs = refs[:layers], refs[layers:]
    mix_refs, refs = refs[: layers - 1], refs[layers - 1 :]
    grad_ref, gw_proj_ref, gw_out_ref, last_mix_ref, low_ref, high_ref = refs[:6]
    bufs = dict(zip(names, refs[6:]))
    width = rows_ref.shape[1]
    masks = head_masks(width)
    place(target_ref, rows_ref, hidden_refs[0], low_ref, high_ref)
    for layer in range(layers):
        last = layer == layers - 1
        weight = weights_ref.at[layer]
        mix_ref = last_mix_ref if last else mix_refs[layer]
        project(hidden_refs[layer], weight, bufs, masks, last)
        attend(mix_ref, bufs, len(masks))
        if not last:
            finish_forward(
                hidden_refs[layer], mix_ref, weight, bufs["gate"], hidden_refs[layer + 1]
            )
    backward(
        hidden_refs[-1],
        cot_ref,
        grad_ref,
        weights_ref.at[layers - 1],
        last_mix_ref,
        gw_proj_ref,
        gw_out_ref,
        bufs,
        masks,
        (here_ref[0], here_ref[1]),
        False,
    )


def place(target_ref, rows_ref, out_ref, low_ref, high_ref):
    length = out_ref.shape[0]
    lanes = 128
    for at in range(0, length, lanes):
        rows = slice(at, at + lanes)
        wanted = as_column(target_ref[:, rows]).astype(jnp.int32)
        wanted = jnp.broadcast_to(wanted, (lanes, lanes))
        high_ref[rows] = (wanted >> 7).astype(F32).astype(BF16)
        lane_row = lax.broadcasted_iota(jnp.int32, (lanes, lanes), 1)
        low_ref[rows] = ((wanted & (lanes - 1)) == lane_row).astype(F32).astype(BF16)
    out_ref[...] = jnp.zeros(out_ref.shape, BF16)

    def step(index, carry):
        low, high = low_ref[...], high_ref[...]
        none = jnp.zeros_like(low)
        hot = [
            jnp.where(high == (2 * index + side).astype(F32).astype(BF16), low, none)
            for side in range(2)
        ]
        chunk = rows_ref[rows_at(index, 2 * lanes)]
        out_ref[...] += nn_dot(jnp.concatenate(hot, axis=1), chunk).astype(BF16)
        return carry

    lax.fori_loop(0, rows_ref.shape[0] // (2 * lanes), step, 0)


def in_memory(count):
    whole = pl.BlockSpec(memory_space=pltpu.VMEM)
    return [pl.BlockSpec(memory_space=pltpu.SMEM)] + [whole] * (count - 1)


def run_top(here, target, rows, weights, cotangent, shards, peers):
    layers = weights.shape[0]
    length, width = cotangent.shape
    buffers = layer_buffers(length, width)
    hidden = jax.ShapeDtypeStruct((length, width), BF16)
    wide = jax.ShapeDtypeStruct((length, width), F32)
    return pl.pallas_call(
        functools.partial(top_kernel, tuple(buffers), layers),
        in_specs=in_memory(5),
        out_shape=[hidden] * layers
        + [wide] * (layers - 1)
        + [wide]
        + weight_shapes(width, shards, peers),
        scratch_shapes=[pltpu.VMEM((length, width), F32)]
        + [pltpu.VMEM((length, 128), BF16)] * 2
        + list(buffers.values()),
        compiler_params=pltpu.CompilerParams(vmem_limit_bytes=62 << 20),
        name="forward_and_last_backward",
    )(here, target, rows, weights, cotangent)


def lower_kernel(
    names, layer, here_ref, target_ref, hidden_ref, mix_ref, weights_ref, grad_ref, out_ref, gw_proj_ref, gw_out_ref, done_ref, *refs
):
    bufs = dict(zip(names, refs))
    masks = head_masks(hidden_ref.shape[1])
    weight = weights_ref.at[layer]
    project(hidden_ref, weight, bufs, masks, True)
    first = layer == 0
    backward(
        hidden_ref,
        grad_ref,
        done_ref if first else out_ref,
        weight,
        mix_ref,
        gw_proj_ref,
        gw_out_ref,
        bufs,
        masks,
        (here_ref[0], here_ref[1]),
        True,
    )
    if not first:
        return
    length = hidden_ref.shape[0]

    target = jnp.broadcast_to(target_ref[...], (BLOCK, length))
    slot_row = lax.broadcasted_iota(jnp.int32, (BLOCK, length), 0)
    low = ((target & (BLOCK - 1)) == slot_row).astype(F32).astype(BF16)
    high = (target >> (BLOCK.bit_length() - 1)).astype(F32).astype(BF16)
    none = jnp.zeros_like(low)
    group = 4 * BLOCK

    def send(index, carry):
        hot = [
            jnp.where(high == (4 * index + at).astype(F32).astype(BF16), low, none)
            for at in range(4)
        ]
        out_ref[rows_at(index, group)] = nn_dot(
            jnp.concatenate(hot, axis=0), done_ref[...]
        ).astype(BF16)
        return carry

    lax.fori_loop(0, out_ref.shape[0] // group, send, 0)


def run_lower(layer, here, target, hidden, mix, weights, gradient, slots, shards, peers):
    length, width = hidden.shape
    buffers = layer_buffers(length, width)
    result = (
        jax.ShapeDtypeStruct((slots, width), BF16)
        if layer == 0
        else jax.ShapeDtypeStruct((length, width), F32)
    )
    return pl.pallas_call(
        functools.partial(lower_kernel, tuple(buffers), layer),
        in_specs=in_memory(6),
        out_shape=[result] + weight_shapes(width, shards, peers),
        scratch_shapes=[pltpu.VMEM((length, width), BF16)] + list(buffers.values()),
        compiler_params=pltpu.CompilerParams(vmem_limit_bytes=62 << 20),
        name="lower_backward",
    )(here, target, hidden, mix, weights, gradient)


def local(item_table, item_owner, item_row, staleness, w_proj, w_out, out_grad):
    fsdp_count = lax.axis_size("fsdp")
    emb_count = lax.axis_size("emb")
    owners = fsdp_count * emb_count
    length = item_row.shape[1]
    capacity = 2 * length // owners
    width = item_table.shape[1]
    layer_count, shard_rows, _ = w_proj.shape
    slots = owners * capacity
    both = ("fsdp", "emb")
    weights = gather_weights(w_proj, w_out)
    target, request = slot_index(item_owner.reshape(1, length), item_row, owners, capacity)
    requested = swap(request, both)
    looked_up, asked = look_up(requested.reshape(owners, capacity), item_table)
    returned = swap(looked_up.reshape(owners, capacity, width), both)
    returned = returned.reshape(slots, width)
    here = jnp.stack([lax.axis_index("fsdp"), lax.axis_index("emb")]).astype(jnp.int32)
    norm_scale = (owners * length) ** (-0.5)
    outs = run_top(here, target, returned, weights, out_grad[0], fsdp_count, emb_count)
    hiddens, mixes = outs[:layer_count], outs[layer_count : 2 * layer_count - 1]
    gradient, gw_proj, gw_out = outs[2 * layer_count - 1 :]
    planes = [plane_sum_whole(weight_pieces(gw_proj, gw_out, False))]
    for layer in reversed(range(layer_count - 1)):
        gradient, gw_proj, gw_out = run_lower(
            layer,
            here,
            target,
            hiddens[layer],
            mixes[layer],
            weights,
            gradient,
            slots,
            fsdp_count,
            emb_count,
        )
        pieces = weight_pieces(gw_proj, gw_out, True)
        planes.insert(0, plane_sum_halving(pieces))
    incoming = swap(gradient.reshape(owners, capacity, width), both)
    incoming = incoming.reshape(slots, width)
    new_table = update_table(asked, staleness, incoming, item_table)
    every = finish_weights(jnp.stack(planes, axis=1), norm_scale)
    sums = [unpack_weights(every[:, at], shard_rows, width) for at in range(layer_count)]
    return (
        new_table,
        jnp.stack([proj for proj, _ in sums]),
        jnp.stack([out for _, out in sums]),
    )


def solution(mesh):
    return jax.shard_map(
        local,
        mesh=mesh,
        in_specs=(
            P(("fsdp", "emb"), None),
            P(("fsdp", "emb"), None, None),
            P(("fsdp", "emb"), None),
            P(("fsdp", "emb")),
            P(None, "fsdp", None),
            P(None, "fsdp", None),
            P(("fsdp", "emb"), None, None),
        ),
        out_specs=(P(("fsdp", "emb"), None), P(None, "fsdp", None), P(None, "fsdp", None)),
        check_vma=False,
    )
```

```python
import functools

import jax
import jax.numpy as jnp
from jax import lax
from jax.experimental import pallas as pl
from jax.experimental.pallas import tpu as pltpu
from jax.sharding import PartitionSpec as P

DH = 64
EPSILON = 1e-05
F32 = jnp.float32
BF16 = jnp.bfloat16


def nt_dot(a, b):
    return lax.dot_general(a, b, (((1,), (1,)), ((), ())), preferred_element_type=F32)


def nn_dot(a, b):
    return jnp.dot(a, b, preferred_element_type=F32)


def as_column(row):
    side = row.shape[1]
    same = lax.broadcasted_iota(jnp.int32, (side, side), 0) == lax.broadcasted_iota(
        jnp.int32, (side, side), 1
    )
    return jnp.sum(jnp.where(same, row.astype(F32), 0.0), axis=1, keepdims=True)


def index_kernel(owner_ref, row_ref, target_ref, request_ref):
    owners, capacity = request_ref.shape
    length = owner_ref.shape[1]
    lane = 128
    owner = owner_ref[...]
    member = (lax.broadcasted_iota(jnp.int32, (owners, length), 0) == owner).astype(F32)
    blocks = [member[:, at : at + lane] for at in range(0, length, lane)]
    stacked = jnp.concatenate(blocks, axis=0).astype(BF16)
    upper = (
        lax.broadcasted_iota(jnp.int32, (lane, lane), 0)
        < lax.broadcasted_iota(jnp.int32, (lane, lane), 1)
    ).astype(F32).astype(BF16)
    inside = nn_dot(stacked, upper)
    base = jnp.zeros((owners, 1), F32)
    slots = []
    for at, block in enumerate(blocks):
        earlier = inside[at * owners : (at + 1) * owners] + base
        slots.append(jnp.sum(earlier * block, axis=0, keepdims=True))
        base = base + jnp.sum(block, axis=1, keepdims=True)
    slot = jnp.concatenate(slots, axis=1).astype(jnp.int32)
    target_ref[...] = owner * capacity + slot
    value = row_ref[...] + 1
    high = (value >> 6).astype(F32)
    low = (value & 63).astype(F32)
    here = lax.broadcasted_iota(jnp.int32, (capacity, length), 0) == slot
    members = member.astype(BF16)
    high_of = nt_dot(members, jnp.where(here, high, 0.0).astype(BF16))
    low_of = nt_dot(members, jnp.where(here, low, 0.0).astype(BF16))
    request_ref[...] = (high_of * 64.0 + low_of).astype(jnp.int32) - 1


def slot_index(owner, offset, owners, capacity):
    length = owner.shape[1]
    return pl.pallas_call(
        index_kernel,
        out_shape=(
            jax.ShapeDtypeStruct((1, length), jnp.int32),
            jax.ShapeDtypeStruct((owners, capacity), jnp.int32),
        ),
        compiler_params=pltpu.CompilerParams(vmem_limit_bytes=62 << 20),
        name="slot_index",
    )(owner, offset)


def lookup_kernel(request_ref, table_ref, out_ref, asked_ref, low_ref, high_ref):
    owners, capacity = request_ref.shape
    slots = owners * capacity
    lanes = 128
    step = pl.program_id(0)
    some = table_ref.shape[0]

    @pl.when(step == 0)
    def _():
        asked_ref[...] = jnp.concatenate(
            [request_ref[at : at + 1, :] for at in range(owners)], axis=1
        )
        asked = jnp.maximum(request_ref[...] + 1, 0)
        split = jnp.concatenate([(asked >> 6).astype(F32), (asked & 63).astype(F32)], axis=1)
        weight = jnp.where(
            lax.broadcasted_iota(jnp.int32, (2 * capacity, lanes), 0) < capacity, 64.0, 1.0
        ).astype(BF16)
        block = 256

        for index in range(slots // block):
            first = index * block
            slot_of = first + lax.broadcasted_iota(jnp.int32, (block, owners), 0)
            owner_at = lax.broadcasted_iota(jnp.int32, (block, owners), 1)
            pick = (slot_of // capacity == owner_at).astype(F32)
            spread = nn_dot(pick.astype(BF16), split.astype(BF16))
            place_at = lax.rem(
                first + lax.broadcasted_iota(jnp.int32, (block, 2 * capacity), 0), capacity
            )
            lane_at = lax.rem(lax.broadcasted_iota(jnp.int32, (block, 2 * capacity), 1), capacity)
            spread = jnp.where(place_at == lane_at, spread, 0.0).astype(BF16)
            wanted = nn_dot(spread, weight).astype(jnp.int32) - 1
            lane_row = lax.broadcasted_iota(jnp.int32, (block, lanes), 1)
            rows = slice(first, first + block)
            high_ref[rows] = (wanted >> 7).astype(F32).astype(BF16)
            low_ref[rows] = ((wanted & (lanes - 1)) == lane_row).astype(F32).astype(BF16)

    first = step * (some // lanes)

    @pl.when(step == 0)
    def _():
        out_ref[...] = jnp.zeros(out_ref.shape, BF16)

    low, high = low_ref[...], high_ref[...]
    none = jnp.zeros_like(low)
    hot = [
        jnp.where(high == (first + at).astype(F32).astype(BF16), low, none)
        for at in range(some // lanes)
    ]
    chunk = table_ref[...].astype(BF16)
    out_ref[...] += nn_dot(jnp.concatenate(hot, axis=1), chunk).astype(BF16)


def look_up(requested, table):
    owners, capacity = requested.shape
    rows, width = table.shape
    slots = owners * capacity
    some = rows // 2
    return pl.pallas_call(
        lookup_kernel,
        grid=(rows // some,),
        in_specs=[
            pl.BlockSpec((owners, capacity), lambda i: (0, 0)),
            pl.BlockSpec((some, width), lambda i: (i, 0)),
        ],
        out_specs=[
            pl.BlockSpec((slots, width), lambda i: (0, 0)),
            pl.BlockSpec((1, slots), lambda i: (0, 0)),
        ],
        out_shape=[
            jax.ShapeDtypeStruct((slots, width), BF16),
            jax.ShapeDtypeStruct((1, slots), jnp.int32),
        ],
        scratch_shapes=[
            pltpu.VMEM((slots, 128), BF16),
            pltpu.VMEM((slots, 128), BF16),
        ],
        compiler_params=pltpu.CompilerParams(vmem_limit_bytes=62 << 20),
        name="look_up",
    )(requested, table)


def update_kernel(request_ref, stale_ref, incoming_ref, table_ref, out_ref, low_ref, high_ref):
    block = out_ref.shape[0]
    group, slots = low_ref.shape

    @pl.when(pl.program_id(0) == 0)
    def _():
        asked = request_ref[...]
        row = lax.broadcasted_iota(jnp.int32, (group, slots), 0)
        low_ref[...] = ((asked & (group - 1)) == row).astype(F32).astype(BF16)
        high_ref[...] = jnp.broadcast_to((asked >> (group.bit_length() - 1)).astype(F32), high_ref.shape).astype(BF16)

    low = low_ref[...]
    high = jnp.concatenate([high_ref[...]] * (group // high_ref.shape[0]), axis=0)
    none = jnp.zeros_like(low)
    first = pl.program_id(0) * (block // group)
    hot = [
        jnp.where(high == (first + at).astype(F32).astype(BF16), low, none)
        for at in range(block // group)
    ]
    table_grad = nn_dot(jnp.concatenate(hot, axis=0), incoming_ref[...])
    stale = [as_column(stale_ref[0, at : at + 1, :]) for at in range(stale_ref.shape[1])]
    rate = 0.5 / (1.0 + jnp.concatenate(stale, axis=0))
    out_ref[...] = table_ref[...] - rate * table_grad


def update_table(requested, staleness, incoming, table):
    rows, width = table.shape
    slots = incoming.shape[0]
    block, group = 1024, 256
    return pl.pallas_call(
        update_kernel,
        grid=(rows // block,),
        in_specs=[
            pl.BlockSpec((1, slots), lambda i: (0, 0)),
            pl.BlockSpec((1, block // 128, 128), lambda i: (i, 0, 0)),
            pl.BlockSpec((slots, width), lambda i: (0, 0)),
            pl.BlockSpec((block, width), lambda i: (i, 0)),
        ],
        out_specs=pl.BlockSpec((block, width), lambda i: (i, 0)),
        out_shape=jax.ShapeDtypeStruct((rows, width), F32),
        scratch_shapes=[pltpu.VMEM((group, slots), BF16), pltpu.VMEM((16, slots), BF16)],
        compiler_params=pltpu.CompilerParams(vmem_limit_bytes=60 << 20),
        name="update_table",
    )(requested, staleness.reshape(rows // block, block // 128, 128), incoming, table)


def swap(payload, axes):
    return lax.all_to_all(payload, axes, split_axis=0, concat_axis=0, tiled=True)


def axis_bits(name):
    size = lax.axis_size(name)
    return [1 << bit for bit in range(size.bit_length() - 1)]


def trade(payload, name, flip):
    size = lax.axis_size(name)
    return lax.ppermute(payload, name, [(at, at ^ flip) for at in range(size)])


def spread_plane(piece):
    whole = piece[None]
    for bit in reversed(axis_bits("emb")):
        other = trade(whole, "emb", bit)
        upper = (lax.axis_index("emb") & bit) != 0
        first = jnp.where(upper, other, whole)
        second = jnp.where(upper, whole, other)
        whole = jnp.stack([first, second], axis=1).reshape((-1,) + piece.shape)
    return whole


def gather_weights(w_proj, w_out):
    fsdp_count = lax.axis_size("fsdp")
    emb_count = lax.axis_size("emb")
    layers, rows, _ = w_proj.shape
    piece = layers * rows // emb_count
    first = lax.axis_index("emb") * piece
    mine = jnp.concatenate(
        [
            lax.dynamic_slice_in_dim(shard.reshape(layers * rows, -1), first, piece, 0)
            for shard in (w_proj, w_out)
        ],
        axis=1,
    )
    taken = [mine] + [trade(mine, "fsdp", flip) for flip in range(1, fsdp_count)]
    index = lax.axis_index("fsdp")
    across = []
    for want in range(fsdp_count):
        chosen = taken[0]
        for flip in range(1, fsdp_count):
            chosen = jnp.where((index ^ flip) == want, taken[flip], chosen)
        across.append(chosen)
    every = spread_plane(jnp.stack(across))
    per = emb_count // layers
    whole = every.reshape(layers, per, fsdp_count, piece, -1).transpose(0, 2, 1, 3, 4)
    return whole.reshape(layers, fsdp_count * rows, -1)


def turn_bits(index, count):
    bits = count.bit_length() - 1
    return sum(((index >> bit) & 1) << (bits - 1 - bit) for bit in range(bits))


def weight_pieces(gw_proj, gw_out, turned):
    if len(gw_proj.shape) == 4:
        return gw_proj
    fsdp_count = lax.axis_size("fsdp")
    emb_count = lax.axis_size("emb")
    rows = gw_proj.shape[0] // fsdp_count
    cols = gw_proj.shape[1] // emb_count
    proj = gw_proj.reshape(fsdp_count, rows, emb_count, cols).transpose(2, 0, 1, 3)
    out = gw_out.reshape(fsdp_count, emb_count, rows // emb_count, -1, cols)
    out = out.transpose(1, 0, 3, 2, 4).reshape(emb_count, fsdp_count, -1, cols)
    pieces = jnp.concatenate([proj, out], axis=2)
    pieces = jnp.take(pieces, jnp.arange(fsdp_count) ^ lax.axis_index("fsdp"), axis=1)
    if turned:
        order = turn_bits(jnp.arange(emb_count), emb_count) ^ lax.axis_index("emb")
        pieces = jnp.take(pieces, order, axis=0)
    return pieces


def plane_sum_whole(pieces):
    return swap(pieces, "emb").astype(F32).sum(axis=0)


def plane_sum_halving(pieces):
    held = pieces
    for bit in axis_bits("emb"):
        half = held.shape[0] // 2
        got = trade(held[half:].astype(BF16), "emb", bit)
        held = held[:half].astype(F32) + got.astype(F32)
    return held[0]


def finish_weights(planes, scale):
    total = planes[0]
    held = planes.astype(BF16)
    for flip in range(1, planes.shape[0]):
        got = trade(held[flip], "fsdp", flip)
        total = total + got.astype(F32)
    return spread_plane((total * scale).astype(BF16))


def unpack_weights(every, rows, width):
    emb_count = every.shape[0]
    proj = every[:, :rows].transpose(1, 0, 2).reshape(rows, -1)
    out = every[:, rows:].reshape(emb_count, -1, rows // emb_count, every.shape[2])
    out = out.transpose(0, 2, 1, 3).reshape(rows, width)
    return proj.astype(F32), out.astype(F32)


BLOCK = 256


def normalize(value):
    center = value - jnp.mean(value, axis=-1, keepdims=True)
    inverse = lax.rsqrt(jnp.mean(center * center, axis=-1, keepdims=True) + EPSILON)
    return center * inverse, inverse


def norm_back(gradient, normed, inverse):
    return inverse * (
        gradient
        - jnp.mean(gradient, axis=-1, keepdims=True)
        - normed * jnp.mean(gradient * normed, axis=-1, keepdims=True)
    )


def each_block(blocks, step):
    group = 2 if blocks % 2 == 0 else 1

    def some(index, carry):
        for at in range(group):
            step(index * group + at, carry)
        return carry

    lax.fori_loop(0, blocks // group, some, 0)


def rows_at(index, size=BLOCK):
    return pl.ds(pl.multiple_of(index * size, size), size)


def head_masks(width):
    lane = lax.broadcasted_iota(jnp.int32, (1, width), 1) // DH
    return [(lane == head).astype(F32).astype(BF16) for head in range(width // DH)]


def fill_stack(ref, index, value, masks):
    for head, mask in enumerate(masks):
        ref[index, head * BLOCK : (head + 1) * BLOCK, :] = value * mask


def project(hidden_ref, weight, bufs, masks, keep):
    width = hidden_ref.shape[1]
    unit = 0.5 * DH ** (-0.5)

    def step(index, carry):
        rows = rows_at(index)
        normed, _ = normalize(hidden_ref[rows].astype(F32))
        normed = 0.5 * normed
        if keep:
            bufs["normed"][:, rows] = normed.T.astype(BF16)
        half = nn_dot(normed.astype(BF16), weight[:, : 4 * width])
        grown = 1.0 + jnp.tanh(half)
        out = (half * grown).astype(BF16)
        if keep:
            grown = grown.astype(BF16)
            bufs["slope"][rows] = grown + out * (2.0 - grown)
        values = out[:, width : 2 * width]
        queries = out[:, 2 * width : 3 * width] * BF16(unit)
        keys = out[:, 3 * width :]
        bufs["gate"][rows] = out[:, :width]
        bufs["keys"][rows] = keys
        bufs["queries"][rows] = queries
        fill_stack(bufs["q_stack"], index, queries, masks)
        fill_stack(bufs["v_stack"], index, values, masks)
        if keep:
            fill_stack(bufs["k_stack"], index, keys, masks)
            bufs["keys_t"][:, rows] = (keys * BF16(unit)).T
        return carry

    each_block(hidden_ref.shape[0] // BLOCK, step)


def attend(mix_ref, bufs, heads):
    blocks = mix_ref.shape[0] // BLOCK
    ahead = lax.broadcasted_iota(jnp.int32, (BLOCK, BLOCK), 1) - lax.broadcasted_iota(
        jnp.int32, (BLOCK, BLOCK), 0
    )

    def clear(index, carry):
        mix_ref[rows_at(index)] = jnp.zeros((BLOCK, mix_ref.shape[1]), F32)
        return carry

    lax.fori_loop(0, blocks, clear, 0)

    def pair(at, to):
        keys = bufs["keys"][rows_at(to)]
        visible = (ahead <= (at - to) * BLOCK).astype(F32).astype(BF16)
        parts = []
        halves = nt_dot(bufs["q_stack"][at], keys).astype(BF16)
        for head in range(heads):
            half = halves[head * BLOCK : (head + 1) * BLOCK]
            parts.append(half * visible * (1.0 + jnp.tanh(half)))
        return nn_dot(jnp.concatenate(parts, axis=1), bufs["v_stack"][to])

    def add(at, to, total):
        mix_ref[rows_at(at)] += total

    each_pair(blocks, pair, add)


def each_pair(blocks, pair, add):
    count = blocks * (blocks + 1) // 2
    group = 5 if count % 5 == 0 else 1

    def step(index, place):
        at, to = place
        work = []
        for _ in range(group):
            work.append((at, to, pair(at, to)))
            done = to == at
            to = jnp.where(done, 0, to + 1)
            at = jnp.where(done, at + 1, at)
        for item in work:
            add(*item)
        return at, to

    lax.fori_loop(0, count // group, step, (jnp.int32(0), jnp.int32(0)))


def finish_forward(hidden_ref, mix_ref, weight, gate_ref, next_ref):
    width = hidden_ref.shape[1]

    def step(index, carry):
        rows = rows_at(index)
        mixed, _ = normalize(mix_ref[rows])
        gated = (mixed * gate_ref[rows].astype(F32)).astype(BF16)
        branch = nn_dot(gated, weight[:, 4 * width :])
        next_ref[rows] = (hidden_ref[rows].astype(F32) + branch).astype(BF16)
        return carry

    lax.fori_loop(0, hidden_ref.shape[0] // BLOCK, step, 0)


def backward(hidden_ref, grad_in, grad_out, weight, mix_ref, gw_proj_ref, gw_out_ref, bufs, masks, here, flip):
    length, width = hidden_ref.shape
    heads = len(masks)
    blocks = length // BLOCK
    slope_ref, gpre_ref, gm_ref = bufs["slope"], bufs["gpre"], bufs["gm"]

    def enter(index, carry):
        rows = rows_at(index)
        gradient = grad_in[rows].astype(BF16)
        mixed, inverse = normalize(mix_ref[rows])
        gate = bufs["gate"][rows].astype(F32)
        gated = mixed * gate
        bufs["gated"][:, rows] = gated.T.astype(BF16)
        grad_gated = nt_dot(gradient, weight[:, 4 * width :])
        gpre_ref[rows, :width] = (grad_gated * mixed).astype(BF16) * slope_ref[rows, :width]
        grad_mix = norm_back(grad_gated * gate, mixed, inverse).astype(BF16)
        gm_ref[rows] = grad_mix
        fill_stack(bufs["g_stack"], index, grad_mix, masks)
        bufs["gq"][:, rows] = jnp.zeros((width, BLOCK), F32)
        bufs["gv"][rows] = jnp.zeros((BLOCK, width), F32)
        bufs["gk"][rows] = jnp.zeros((BLOCK, width), F32)
        bufs["round"][rows] = gradient
        return carry

    each_block(blocks, enter)
    store_out_pieces(gw_out_ref, gw_proj_ref, nn_dot(bufs["gated"][...], bufs["round"][...]), here, flip)
    ahead = lax.broadcasted_iota(jnp.int32, (BLOCK, BLOCK), 0) - lax.broadcasted_iota(
        jnp.int32, (BLOCK, BLOCK), 1
    )

    def pair(at, to):
        keys_at, cols = rows_at(to), rows_at(at)
        visible = (ahead <= (at - to) * BLOCK).astype(F32).astype(BF16)
        attns, grads, turned = [], [], []
        halves = nt_dot(bufs["k_stack"][to], bufs["queries"][cols]).astype(BF16)
        grad_attns = nt_dot(bufs["v_stack"][to], gm_ref[cols]).astype(BF16)
        for head in range(heads):
            span = slice(head * BLOCK, (head + 1) * BLOCK)
            half = halves[span]
            turn = jnp.tanh(half)
            grown = 1.0 + turn
            attn = half * grown
            attns.append(attn * visible)
            grads.append(grad_attns[span] * visible * (grown + attn * (1.0 - turn)))
            place = slice(head * DH, (head + 1) * DH)
            turned.append(nn_dot(bufs["keys_t"][place, keys_at], grads[-1]))
        return (
            nn_dot(jnp.concatenate(attns, axis=1), bufs["g_stack"][at]),
            nn_dot(jnp.concatenate(grads, axis=1), bufs["q_stack"][at]),
            turned,
        )

    def add(at, to, totals):
        keys_at, cols = rows_at(to), rows_at(at)
        bufs["gv"][keys_at] += totals[0]
        bufs["gk"][keys_at] += totals[1]
        for head in range(heads):
            bufs["gq"][head * DH : (head + 1) * DH, cols] += totals[2][head]

    each_pair(blocks, pair, add)

    def leave(index, carry):
        rows = rows_at(index)
        for at, grad in enumerate((bufs["gv"][rows], bufs["gq"][:, rows].T, bufs["gk"][rows])):
            cols = slice((at + 1) * width, (at + 2) * width)
            gpre_ref[rows, cols] = grad.astype(BF16) * slope_ref[rows, cols]
        grad_normed = nt_dot(gpre_ref[rows, :], weight[:, : 4 * width])
        normed, inverse = normalize(hidden_ref[rows].astype(F32))
        gradient = grad_in[rows].astype(F32) + norm_back(grad_normed, normed, 0.5 * inverse)
        grad_out[rows] = gradient.astype(grad_out.dtype)
        return carry

    each_block(blocks, leave)

    def weigh(index, carry):
        cols = rows_at(index)
        grad = nn_dot(bufs["normed"][...], gpre_ref[:, cols]).astype(BF16)
        if len(gw_proj_ref.shape) == 2:
            gw_proj_ref[:, cols] = grad
            return carry
        peers, shards, _, lanes = gw_proj_ref.shape
        deep = width // shards
        for part in range(BLOCK // lanes):
            for shard in range(shards):
                slot = peer_slot(index * (BLOCK // lanes) + part, peers, here, flip)
                gw_proj_ref[slot, shard ^ here[0], :deep, :] = grad[
                    shard * deep : (shard + 1) * deep, part * lanes : (part + 1) * lanes
                ]
        return carry

    each_block(4 * width // BLOCK, weigh)


def peer_slot(peer, peers, here, flip):
    return turn_bits(peer ^ here[1], peers) if flip else peer


def store_out_pieces(gw_out_ref, gw_proj_ref, grad, here, flip):
    if len(gw_proj_ref.shape) == 2:
        gw_out_ref[...] = grad.astype(BF16)
        return
    peers, shards, rows, lanes = gw_proj_ref.shape
    width = grad.shape[0]
    deep = width // shards
    some = deep // peers
    for shard in range(shards):
        for peer in range(peers):
            first = shard * deep + peer * some
            piece = [
                grad[first : first + some, at : at + lanes] for at in range(0, width, lanes)
            ]
            gw_proj_ref[peer_slot(peer, peers, here, flip), shard ^ here[0], deep:rows, :] = jnp.concatenate(piece, axis=0).astype(BF16)
    gw_out_ref[...] = jnp.zeros(gw_out_ref.shape, BF16)


def weight_shapes(width, shards, peers):
    deep = width // shards
    lanes = 4 * width // peers
    if lanes == 128 and deep // peers == 8 and deep % 16 == 0:
        rows = deep + deep // peers * width // lanes
        return [
            jax.ShapeDtypeStruct((peers, shards, rows, lanes), BF16),
            jax.ShapeDtypeStruct((8, 128), BF16),
        ]
    return [
        jax.ShapeDtypeStruct((width, 4 * width), BF16),
        jax.ShapeDtypeStruct((width, width), BF16),
    ]


def layer_buffers(length, width):
    heads = width // DH
    blocks = length // BLOCK
    stack = pltpu.VMEM((blocks, heads * BLOCK, width), BF16)
    plain = pltpu.VMEM((length, width), BF16)
    turned = pltpu.VMEM((width, length), BF16)
    return dict(
        slope=pltpu.VMEM((length, 4 * width), BF16),
        gpre=pltpu.VMEM((length, 4 * width), BF16),
        normed=turned,
        gated=turned,
        keys_t=turned,
        gq=pltpu.VMEM((width, length), F32),
        gv=pltpu.VMEM((length, width), F32),
        gk=pltpu.VMEM((length, width), F32),
        gate=plain,
        keys=plain,
        queries=plain,
        gm=plain,
        round=plain,
        q_stack=stack,
        k_stack=stack,
        v_stack=stack,
        g_stack=stack,
    )


def top_kernel(names, layers, here_ref, target_ref, rows_ref, weights_ref, cot_ref, *refs):
    hidden_refs, refs = refs[:layers], refs[layers:]
    mix_refs, refs = refs[: layers - 1], refs[layers - 1 :]
    grad_ref, gw_proj_ref, gw_out_ref, last_mix_ref, low_ref, high_ref = refs[:6]
    bufs = dict(zip(names, refs[6:]))
    width = rows_ref.shape[1]
    masks = head_masks(width)
    place(target_ref, rows_ref, hidden_refs[0], low_ref, high_ref)
    for layer in range(layers):
        last = layer == layers - 1
        weight = weights_ref.at[layer]
        mix_ref = last_mix_ref if last else mix_refs[layer]
        project(hidden_refs[layer], weight, bufs, masks, last)
        attend(mix_ref, bufs, len(masks))
        if not last:
            finish_forward(
                hidden_refs[layer], mix_ref, weight, bufs["gate"], hidden_refs[layer + 1]
            )
    backward(
        hidden_refs[-1],
        cot_ref,
        grad_ref,
        weights_ref.at[layers - 1],
        last_mix_ref,
        gw_proj_ref,
        gw_out_ref,
        bufs,
        masks,
        (here_ref[0], here_ref[1]),
        False,
    )


def place(target_ref, rows_ref, out_ref, low_ref, high_ref):
    length = out_ref.shape[0]
    lanes = 128
    for at in range(0, length, lanes):
        rows = slice(at, at + lanes)
        wanted = as_column(target_ref[:, rows]).astype(jnp.int32)
        wanted = jnp.broadcast_to(wanted, (lanes, lanes))
        high_ref[rows] = (wanted >> 7).astype(F32).astype(BF16)
        lane_row = lax.broadcasted_iota(jnp.int32, (lanes, lanes), 1)
        low_ref[rows] = ((wanted & (lanes - 1)) == lane_row).astype(F32).astype(BF16)
    out_ref[...] = jnp.zeros(out_ref.shape, BF16)

    def step(index, carry):
        low, high = low_ref[...], high_ref[...]
        none = jnp.zeros_like(low)
        hot = [
            jnp.where(high == (2 * index + side).astype(F32).astype(BF16), low, none)
            for side in range(2)
        ]
        chunk = rows_ref[rows_at(index, 2 * lanes)]
        out_ref[...] += nn_dot(jnp.concatenate(hot, axis=1), chunk).astype(BF16)
        return carry

    each_block(rows_ref.shape[0] // (2 * lanes), step)


def in_memory(count):
    whole = pl.BlockSpec(memory_space=pltpu.VMEM)
    return [pl.BlockSpec(memory_space=pltpu.SMEM)] + [whole] * (count - 1)


def run_top(here, target, rows, weights, cotangent, shards, peers):
    layers = weights.shape[0]
    length, width = cotangent.shape
    buffers = layer_buffers(length, width)
    hidden = jax.ShapeDtypeStruct((length, width), BF16)
    wide = jax.ShapeDtypeStruct((length, width), F32)
    return pl.pallas_call(
        functools.partial(top_kernel, tuple(buffers), layers),
        in_specs=in_memory(5),
        out_shape=[hidden] * layers
        + [wide] * (layers - 1)
        + [wide]
        + weight_shapes(width, shards, peers),
        scratch_shapes=[pltpu.VMEM((length, width), F32)]
        + [pltpu.VMEM((length, 128), BF16)] * 2
        + list(buffers.values()),
        compiler_params=pltpu.CompilerParams(vmem_limit_bytes=62 << 20),
        name="forward_and_last_backward",
    )(here, target, rows, weights, cotangent)


def lower_kernel(
    names, layer, here_ref, target_ref, hidden_ref, mix_ref, weights_ref, grad_ref, out_ref, gw_proj_ref, gw_out_ref, done_ref, *refs
):
    bufs = dict(zip(names, refs))
    masks = head_masks(hidden_ref.shape[1])
    weight = weights_ref.at[layer]
    project(hidden_ref, weight, bufs, masks, True)
    first = layer == 0
    backward(
        hidden_ref,
        grad_ref,
        done_ref if first else out_ref,
        weight,
        mix_ref,
        gw_proj_ref,
        gw_out_ref,
        bufs,
        masks,
        (here_ref[0], here_ref[1]),
        True,
    )
    if not first:
        return
    length = hidden_ref.shape[0]

    target = jnp.broadcast_to(target_ref[...], (BLOCK, length))
    slot_row = lax.broadcasted_iota(jnp.int32, (BLOCK, length), 0)
    low = ((target & (BLOCK - 1)) == slot_row).astype(F32).astype(BF16)
    high = (target >> (BLOCK.bit_length() - 1)).astype(F32).astype(BF16)
    none = jnp.zeros_like(low)
    group = 4 * BLOCK

    def send(index, carry):
        hot = [
            jnp.where(high == (4 * index + at).astype(F32).astype(BF16), low, none)
            for at in range(4)
        ]
        out_ref[rows_at(index, group)] = nn_dot(
            jnp.concatenate(hot, axis=0), done_ref[...]
        ).astype(BF16)
        return carry

    lax.fori_loop(0, out_ref.shape[0] // group, send, 0)


def run_lower(layer, here, target, hidden, mix, weights, gradient, slots, shards, peers):
    length, width = hidden.shape
    buffers = layer_buffers(length, width)
    result = (
        jax.ShapeDtypeStruct((slots, width), BF16)
        if layer == 0
        else jax.ShapeDtypeStruct((length, width), F32)
    )
    return pl.pallas_call(
        functools.partial(lower_kernel, tuple(buffers), layer),
        in_specs=in_memory(6),
        out_shape=[result] + weight_shapes(width, shards, peers),
        scratch_shapes=[pltpu.VMEM((length, width), BF16)] + list(buffers.values()),
        compiler_params=pltpu.CompilerParams(vmem_limit_bytes=62 << 20),
        name="lower_backward",
    )(here, target, hidden, mix, weights, gradient)


def local(item_table, item_owner, item_row, staleness, w_proj, w_out, out_grad):
    fsdp_count = lax.axis_size("fsdp")
    emb_count = lax.axis_size("emb")
    owners = fsdp_count * emb_count
    length = item_row.shape[1]
    capacity = 2 * length // owners
    width = item_table.shape[1]
    layer_count, shard_rows, _ = w_proj.shape
    slots = owners * capacity
    both = ("fsdp", "emb")
    weights = gather_weights(w_proj, w_out)
    target, request = slot_index(item_owner.reshape(1, length), item_row, owners, capacity)
    requested = swap(request, both)
    looked_up, asked = look_up(requested.reshape(owners, capacity), item_table)
    returned = swap(looked_up.reshape(owners, capacity, width), both)
    returned = returned.reshape(slots, width)
    here = jnp.stack([lax.axis_index("fsdp"), lax.axis_index("emb")]).astype(jnp.int32)
    norm_scale = (owners * length) ** (-0.5)
    outs = run_top(here, target, returned, weights, out_grad[0], fsdp_count, emb_count)
    hiddens, mixes = outs[:layer_count], outs[layer_count : 2 * layer_count - 1]
    gradient, gw_proj, gw_out = outs[2 * layer_count - 1 :]
    planes = [plane_sum_whole(weight_pieces(gw_proj, gw_out, False))]
    for layer in reversed(range(layer_count - 1)):
        gradient, gw_proj, gw_out = run_lower(
            layer,
            here,
            target,
            hiddens[layer],
            mixes[layer],
            weights,
            gradient,
            slots,
            fsdp_count,
            emb_count,
        )
        pieces = weight_pieces(gw_proj, gw_out, True)
        planes.insert(0, plane_sum_halving(pieces))
    incoming = swap(gradient.reshape(owners, capacity, width), both)
    incoming = incoming.reshape(slots, width)
    new_table = update_table(asked, staleness, incoming, item_table)
    every = finish_weights(jnp.stack(planes, axis=1), norm_scale)
    sums = [unpack_weights(every[:, at], shard_rows, width) for at in range(layer_count)]
    return (
        new_table,
        jnp.stack([proj for proj, _ in sums]),
        jnp.stack([out for _, out in sums]),
    )


def solution(mesh):
    return jax.shard_map(
        local,
        mesh=mesh,
        in_specs=(
            P(("fsdp", "emb"), None),
            P(("fsdp", "emb"), None, None),
            P(("fsdp", "emb"), None),
            P(("fsdp", "emb")),
            P(None, "fsdp", None),
            P(None, "fsdp", None),
            P(("fsdp", "emb"), None, None),
        ),
        out_specs=(P(("fsdp", "emb"), None), P(None, "fsdp", None), P(None, "fsdp", None)),
        check_vma=False,
    )
```
